32 devices in a mesh: snap: 2 (over x), inner: 16 (over z, y, core).
Axes of the slice: x: 2, y: 2, z: 4, core: 2. Of those that a mesh axis runs over, the one named last changes fastest.
Arguments:
- vertices: float32 [16384, 256], P(('snap', 'inner')), parts along dimension 0, may hold values from -0.75 to 0.75
- vertex_moments: float32 [16384, 256], P(('snap', 'inner')), parts along dimension 0, may hold values from 0.1 to 2
- contexts: float32 [32768, 256], P(('snap', 'inner')), parts along dimension 0, may hold values from -0.75 to 0.75
- context_moments: float32 [32768, 256], P(('snap', 'inner')), parts along dimension 0, may hold values from 0.1 to 2
- edge_counts: int32 [3, 512, 32768], P(None, None, ('snap', 'inner')), parts along dimension 2, may hold values from 0 to 4
- negative_weights: int32 [3, 32768], P(None, ('snap', 'inner')), parts along dimension 1, may hold values from 1 to 6
Outputs:
- vertex_out: float32 [16384, 256], P(('snap', 'inner')), parts along dimension 0
- vertex_moments_out: float32 [16384, 256], P(('snap', 'inner')), parts along dimension 0
- context_out: float32 [32768, 256], P(('snap', 'inner')), parts along dimension 0
- context_moments_out: float32 [32768, 256], P(('snap', 'inner')), parts along dimension 0
The draws below stay inside these ranges and needn't reach their ends.
There are 2 independent parts, one for each index of `snap`. The reference program is written for one: setup_inputs(seed, part) draws one part's arguments, and reference() takes and returns one part's arrays. A program takes and returns all parts, laid end to end along the dimension named above; each array names one. Nothing has to cross between parts.
All inputs are finite; a program needn't handle non-finite values.
Results may differ from the reference program's by a relative error of at most 0.0001.
Values sent between devices are 32-bit elements; how exact they have to be, the bound alone decides.
A program may use at most 64 MiB of HBM per device.

```python
import math
import jax
import jax.numpy as jnp
from jax import lax

D = 256
VB = 512
CB = 1024
STEPS = 3
VERTS = 8192
CONTEXTS = 16384
N_INNER = 16


def touch_ends(result, key, least, largest):
    dims = result.shape
    place = [jax.random.randint(jax.random.fold_in(key, axis), (), 0, dims[axis]) for axis in range(len(dims))]
    result = result.at[tuple(place)].set(least)
    longest = dims.index(max(dims))
    place[longest] = (place[longest] + 1) % dims[longest]
    return result.at[tuple(place)].set(largest)


def levels(rng, dims, cuts, smallest, top_value):
    factor_of = 1.0
    for axis_at, parts in cuts:
        steps = jax.random.uniform(jax.random.fold_in(jax.random.fold_in(rng, 6), axis_at), (parts,), jnp.float32, smallest / len(cuts), top_value / len(cuts))
        factor_of = factor_of * jnp.repeat(jnp.exp(steps), dims[axis_at] // parts).reshape((-1,) + (1,) * (len(dims) - 1 - axis_at))
    return factor_of


def gaussian(own_key, shape, deviation, limit, shards=(), dtype=jnp.bfloat16):
    factor_of = levels(own_key, shape, shards, -0.22, 0.18) if shards else 1.0
    result = jax.random.normal(own_key, shape, jnp.float32) * deviation * factor_of
    return jnp.minimum(jnp.maximum(result, -limit), limit).astype(dtype)


def setup_inputs(seed: int = 0, part: int = 0) -> dict:
    key_of = jax.random.split(jax.random.key(seed), 7)
    part_keys = jax.random.split(jax.random.fold_in(key_of[6], part), 7)
    vertices = gaussian(part_keys[0], (VERTS, D), 0.125, 0.75, ((0, 16),), jnp.float32)
    vertex_moments = jnp.clip(jnp.exp(math.log(2.0) - 2.9957323 * jax.random.uniform(part_keys[1], (VERTS, D), jnp.float32) ** levels(part_keys[1], (VERTS, D), ((0, 16),), -0.2, 0.2)), 0.1, 2.0)
    contexts = gaussian(part_keys[2], (CONTEXTS, D), 0.125, 0.75, ((0, 16),), jnp.float32)
    context_moments = jnp.clip(jnp.exp(math.log(2.0) - 2.9957323 * jax.random.uniform(part_keys[3], (CONTEXTS, D), jnp.float32) ** levels(part_keys[3], (CONTEXTS, D), ((0, 16),), -0.2, 0.2)), 0.1, 2.0)
    edge_counts = touch_ends(jax.random.randint(part_keys[4], (STEPS, VB, CONTEXTS), 0, 5), jax.random.fold_in(part_keys[4], 1), 0, 4).astype(jnp.int32)
    negative_weights = touch_ends(jax.random.randint(part_keys[5], (STEPS, CONTEXTS), 1, 7), jax.random.fold_in(part_keys[5], 1), 1, 6).astype(jnp.int32)
    return {"vertices": vertices, "vertex_moments": vertex_moments, "contexts": contexts, "context_moments": context_moments, "edge_counts": edge_counts, "negative_weights": negative_weights}


def one_step(ublk, gblk, cblk, hblk, counts, negs):
    scores = jnp.einsum('bvd,bcd->bvc', ublk, cblk, precision=lax.Precision.HIGHEST)
    ecount = counts.astype(jnp.float32)
    resid = (ecount + negs.astype(jnp.float32)[:, None, :]) * jax.nn.sigmoid(scores) - ecount
    grad_u = jnp.einsum('bvc,bcd->bvd', resid, cblk, precision=lax.Precision.HIGHEST)
    grad_c = jnp.einsum('bvc,bvd->bcd', resid, ublk, precision=lax.Precision.HIGHEST)
    gblk = gblk + grad_u * grad_u
    ublk = ublk - 0.05 * grad_u / jnp.sqrt(gblk)
    hblk = hblk + grad_c * grad_c
    cblk = cblk - 0.05 * grad_c / jnp.sqrt(hblk)
    return (ublk, gblk, cblk, hblk)

def reference(vertices, vertex_moments, contexts, context_moments, edge_counts, negative_weights):
    blocks = N_INNER
    ublk = vertices.reshape(blocks, VB, D)
    gblk = vertex_moments.reshape(blocks, VB, D)
    cblk = contexts.reshape(blocks, CB, D)
    hblk = context_moments.reshape(blocks, CB, D)
    for step in range(STEPS):
        counts = jnp.transpose(edge_counts[step].reshape(VB, blocks, CB), (1, 0, 2))
        negs = negative_weights[step].reshape(blocks, CB)
        moved_u = jnp.roll(ublk, step, axis=0)
        moved_g = jnp.roll(gblk, step, axis=0)
        moved_u, moved_g, cblk, hblk = one_step(moved_u, moved_g, cblk, hblk, counts, negs)
        ublk = jnp.roll(moved_u, -step, axis=0)
        gblk = jnp.roll(moved_g, -step, axis=0)
    return (ublk.reshape(VERTS, D), gblk.reshape(VERTS, D), cblk.reshape(CONTEXTS, D), hblk.reshape(CONTEXTS, D))
```

```python
import functools

import jax
import jax.numpy as jnp
from jax import lax
from jax.experimental import pallas as pl
from jax.experimental.pallas import tpu as pltpu
from jax.sharding import PartitionSpec as P

F32 = jnp.float32
BF16 = jnp.bfloat16
MESH = pl.DeviceIdType.MESH
NN = (((1,), (0,)), ((), ()))
NT = (((1,), (1,)), ((), ()))
TN = (((0,), (0,)), ((), ()))
U1, G1, U2, D1, D2 = range(5)


def split(x):
    hi = x.astype(BF16)
    return hi, (x - hi.astype(F32)).astype(BF16)


def dot3(a, b, dims):
    dot = functools.partial(lax.dot_general, dimension_numbers=dims, preferred_element_type=F32)
    free = 1 - dims[0][0][0]
    m = a[0].shape[free]
    both = dot(jnp.concatenate(a, axis=free), b[0])
    return both[:m] + (dot(a[0], b[1]) + both[m:])


def kernel(n, chunk, tile, u_hbm, g_hbm, c_hbm, h_hbm, e_hbm, w_hbm, uo, go, co, ho,
           u, g, c, h, e, w, ch, cl, uh, ul, rh, rl, land, out,
           in_sem, e_sem, send_sem, recv_sem, grant):
    me = lax.axis_index("inner")
    hold = n % 4 == 0
    snap = lax.axis_index("snap")
    at = lambda shift: lax.rem(me + shift + n, n)
    vb, cb = u.shape[0], c.shape[0]
    nchunks, ntiles = vb // chunk, cb // tile
    rows = lambda r: pl.ds(pl.multiple_of(r * chunk, chunk), chunk)
    cols = lambda j: pl.ds(pl.multiple_of(j * tile, tile), tile)

    ins = [pltpu.make_async_copy(src, dst, in_sem.at[k])
           for k, (src, dst) in enumerate(((c_hbm, c), (u_hbm, u), (g_hbm, g), (h_hbm, h), (w_hbm, w)))]

    def counts(step, r):
        return pltpu.make_async_copy(e_hbm.at[step, rows(r)], e.at[step, rows(r)], e_sem.at[step, r])

    ins[0].start()
    ins[1].start()
    ins[4].start()
    counts(0, 0).start()
    ins[2].start()
    for r in range(1, nchunks):
        counts(0, r).start()
    ins[3].start()

    barrier = pltpu.get_barrier_semaphore()
    for shift in (1, -1, 2, -2, -3):
        pl.semaphore_signal(barrier, inc=1, device_id=(snap, at(shift)), device_id_type=MESH)

    def remote(kind, r):
        src = (u, g, out.at[0], out.at[1], out.at[2])[kind]
        to = (1, 1, 1, -1, -2)[kind]
        return pltpu.make_async_remote_copy(
            src_ref=src.at[rows(r)], dst_ref=land.at[kind, rows(r)],
            send_sem=send_sem.at[kind, r], recv_sem=recv_sem.at[kind, r],
            device_id=(snap, at(to)), device_id_type=MESH)

    def each(body):
        def run(r, carry):
            body(r)
            return carry
        lax.fori_loop(0, nchunks, run, 0)

    def each_tile(body):
        def run(j, carry):
            body(j)
            return carry
        lax.fori_loop(0, ntiles, run, 0)

    def gradient(step, r, source):
        counts(step, r).wait()
        two = split(source[rows(r), :])
        uh[rows(r), :], ul[rows(r), :] = two
        scores = dot3(two, (ch[...], cl[...]), NT)
        ecount = e[step, rows(r), :].astype(F32)
        resid = (ecount + w[step:step + 1, :].astype(F32)) * jax.nn.sigmoid(scores) - ecount
        two = split(resid)
        rh[rows(r), :], rl[rows(r), :] = two
        return dot3(two, (ch[...], cl[...]), NN)

    def contexts(step):
        def one(j):
            grad = dot3((rh[:, cols(j)], rl[:, cols(j)]), (uh[...], ul[...]), TN)
            moments = h[cols(j), :] + grad * grad
            value = c[cols(j), :] - 0.05 * grad * lax.rsqrt(moments)
            (h if step < 2 else ho)[cols(j), :] = moments
            (c if step < 2 else co)[cols(j), :] = value
            if step < 2:
                ch[cols(j), :], cl[cols(j), :] = split(value)
        each_tile(one)

    ins[0].wait()

    def prepare(j):
        ch[cols(j), :], cl[cols(j), :] = split(c[cols(j), :])
    each_tile(prepare)
    each(lambda r: counts(1, r).start())
    ins[1].wait()
    ins[4].wait()
    ins[2].wait()

    def step0(r):
        grad = gradient(0, r, u)
        moments = g[rows(r), :] + grad * grad
        u[rows(r), :] = u[rows(r), :] - 0.05 * grad * lax.rsqrt(moments)
        g[rows(r), :] = moments

        @pl.when(r == 0)
        def _():
            pl.semaphore_wait(barrier, 5)
        remote(U1, r).start()
    each(step0)
    each(lambda r: counts(2, r).start())
    each(lambda r: remote(G1, r).start())
    ins[3].wait()
    contexts(0)

    def step1(r):
        remote(U1, r).wait_recv()
        out[1, rows(r), :] = gradient(1, r, land.at[U1])
    each(step1)

    def forward(r):
        remote(G1, r).wait_recv()
        grad = out[1, rows(r), :]
        moments = land[G1, rows(r), :] + grad * grad
        out[0, rows(r), :] = land[U1, rows(r), :] - 0.05 * grad * lax.rsqrt(moments)
        remote(U2, r).start()
    contexts(1)
    each(forward)
    held = hold & (lax.rem(me, 4) < 2)
    free = jnp.logical_not(held)

    @pl.when(free | (lax.rem(me, 2) == 1))
    def _():
        each(lambda r: remote(D1, r).start())

    def step2(r):
        remote(U2, r).wait_recv()

        if hold:
            @pl.when((lax.rem(me, 4) == 2) & (r == nchunks - 3))
            def _():
                for shift in (2, 3):
                    pl.semaphore_signal(grant, inc=1, device_id=(snap, at(shift)), device_id_type=MESH)

        out[2, rows(r), :] = gradient(2, r, land.at[U2])

        @pl.when(free)
        def _():
            remote(D2, r).start()
    each(step2)

    if hold:
        @pl.when(held)
        def _():
            pl.semaphore_wait(grant, 1)

            @pl.when(lax.rem(me, 2) == 0)
            def _():
                each(lambda r: remote(D1, r).start())
            each(lambda r: remote(D2, r).start())
    contexts(2)

    def home(r):
        remote(D1, r).wait_recv()
        grad = land[D1, rows(r), :]
        moments = g[rows(r), :] + grad * grad
        value = u[rows(r), :] - 0.05 * grad * lax.rsqrt(moments)
        remote(D2, r).wait_recv()
        grad = land[D2, rows(r), :]
        moments = moments + grad * grad
        uo[rows(r), :] = value - 0.05 * grad * lax.rsqrt(moments)
        go[rows(r), :] = moments
    each(home)

    def finish(r):
        for kind in range(5):
            remote(kind, r).wait_send()
    each(finish)


def write_out(*refs):
    copies = [pltpu.make_async_copy(refs[k], refs[4 + k], refs[8].at[k]) for k in range(4)]
    for copy in copies:
        copy.start()
    for copy in copies:
        copy.wait()


def per_device(n, vertices, vertex_moments, contexts, context_moments, edge_counts, negative_weights):
    (vb, d), cb = vertices.shape, contexts.shape[0]
    nsteps = edge_counts.shape[0]
    chunk = vb // 4 if vb % 64 == 0 else vb
    tile = cb // 2 if cb % 512 == 0 else cb
    r = vb // chunk
    hbm = pl.BlockSpec(memory_space=pltpu.HBM)
    vmem = pltpu.VMEM
    dma = pltpu.SemaphoreType.DMA
    outs = [vertices, vertex_moments, contexts, context_moments]
    limit = (64 << 20) - sum(a.size * 4 for a in outs) - (160 << 10)
    done = pl.pallas_call(
        functools.partial(kernel, n, chunk, tile),
        out_shape=[vmem(a.shape, F32) for a in outs],
        in_specs=[hbm] * 6,
        out_specs=[pl.BlockSpec(memory_space=vmem)] * 4,
        scratch_shapes=[
            vmem((vb, d), F32), vmem((vb, d), F32), vmem((cb, d), F32), vmem((cb, d), F32),
            vmem((nsteps, vb, cb), jnp.int32), vmem(negative_weights.shape, jnp.int32),
            vmem((cb, d), BF16), vmem((cb, d), BF16),
            vmem((vb, d), BF16), vmem((vb, d), BF16),
            vmem((vb, cb), BF16), vmem((vb, cb), BF16),
            vmem((5, vb, d), F32), vmem((3, vb, d), F32),
            dma((5,)), dma((nsteps, r)), dma((5, r)), dma((5, r)),
            pltpu.SemaphoreType.REGULAR,
        ],
        compiler_params=pltpu.CompilerParams(collective_id=0, has_side_effects=True, vmem_limit_bytes=limit),
    )(vertices, vertex_moments, contexts, context_moments, edge_counts, negative_weights)
    return tuple(pl.pallas_call(
        write_out,
        out_shape=[jax.ShapeDtypeStruct(a.shape, F32) for a in outs],
        in_specs=[pl.BlockSpec(memory_space=vmem)] * 4,
        out_specs=[hbm] * 4,
        scratch_shapes=[dma((4,))],
        compiler_params=pltpu.CompilerParams(vmem_limit_bytes=1 << 20),
    )(*done))


def solution(mesh):
    rows = P(("snap", "inner"), None)
    return jax.shard_map(
        functools.partial(per_device, mesh.shape["inner"]),
        mesh=mesh,
        in_specs=(rows, rows, rows, rows, P(None, None, ("snap", "inner")), P(None, ("snap", "inner"))),
        out_specs=(rows, rows, rows, rows),
        check_vma=False,
    )
```

```python
import functools

import jax
import jax.numpy as jnp
from jax import lax
from jax.experimental import pallas as pl
from jax.experimental.pallas import tpu as pltpu
from jax.sharding import PartitionSpec as P

F32 = jnp.float32
BF16 = jnp.bfloat16
MESH = pl.DeviceIdType.MESH
NN = (((1,), (0,)), ((), ()))
NT = (((1,), (1,)), ((), ()))
TN = (((0,), (0,)), ((), ()))
U1, G1, U2, D1, D2 = range(5)


def split(x):
    hi = x.astype(BF16)
    return hi, (x - hi.astype(F32)).astype(BF16)


def dot3(a, b, dims):
    dot = functools.partial(lax.dot_general, dimension_numbers=dims, preferred_element_type=F32)
    free = 1 - dims[0][0][0]
    m = a[0].shape[free]
    both = dot(jnp.concatenate(a, axis=free), b[0])
    return both[:m] + (dot(a[0], b[1]) + both[m:])


def kernel(n, chunk, tile, u_hbm, g_hbm, c_hbm, h_hbm, e_hbm, w_hbm, uo, go, co, ho,
           u, g, c, h, e, w, ch, cl, uh, ul, rh, rl, land, out,
           in_sem, e_sem, send_sem, recv_sem, grant, via, via_sem):
    me = lax.axis_index("inner")
    hold = n % 4 == 0
    nvia = max(0, min(2, u.shape[0] // chunk - 1, n // 4 - 1)) if hold else 0
    relay = (lax.rem(me, 4) == 0) & (me > 0) & (me <= 4 * nvia)
    snap = lax.axis_index("snap")
    at = lambda shift: lax.rem(me + shift + n, n)
    vb, cb = u.shape[0], c.shape[0]
    nchunks, ntiles = vb // chunk, cb // tile
    rows = lambda r: pl.ds(pl.multiple_of(r * chunk, chunk), chunk)
    cols = lambda j: pl.ds(pl.multiple_of(j * tile, tile), tile)

    ins = [pltpu.make_async_copy(src, dst, in_sem.at[k])
           for k, (src, dst) in enumerate(((c_hbm, c), (u_hbm, u), (g_hbm, g), (h_hbm, h), (w_hbm, w)))]

    def counts(step, r):
        return pltpu.make_async_copy(e_hbm.at[step, rows(r)], e.at[step, rows(r)], e_sem.at[step, r])

    ins[0].start()
    ins[1].start()
    ins[4].start()
    counts(0, 0).start()
    ins[2].start()

    barrier = pltpu.get_barrier_semaphore()
    for shift in (-1, -2, -3):
        pl.semaphore_signal(barrier, inc=1, device_id=(snap, at(shift)), device_id_type=MESH)
    if nvia:
        @pl.when(me == 1)
        def _():
            for k in range(nvia):
                pl.semaphore_signal(barrier, inc=1, device_id=(snap, 4 * (k + 1)), device_id_type=MESH)

        @pl.when(relay)
        def _():
            pl.semaphore_signal(barrier, inc=1, device_id=(snap, 2), device_id_type=MESH)

    def part_of(kind, r, part):
        src = (u, g, out.at[0], out.at[1], out.at[2])[kind]
        to = (1, 1, 1, -1, -2)[kind]
        return pltpu.make_async_remote_copy(
            src_ref=src.at[part], dst_ref=land.at[kind, part],
            send_sem=send_sem.at[kind, r], recv_sem=recv_sem.at[kind, r],
            device_id=(snap, at(to)), device_id_type=MESH)

    def remote(kind, r):
        return part_of(kind, r, rows(r))

    def via_in(r):
        return pltpu.make_async_remote_copy(
            src_ref=out.at[1, rows(r)], dst_ref=via, send_sem=send_sem.at[D1, r], recv_sem=via_sem.at[0],
            device_id=(snap, 4 * (r + 1)), device_id_type=MESH)

    def via_out(r):
        return pltpu.make_async_remote_copy(
            src_ref=via, dst_ref=land.at[D1, rows(r)], send_sem=via_sem.at[1], recv_sem=recv_sem.at[D1, r],
            device_id=(snap, 1), device_id_type=MESH)

    def enter():
        if nvia:
            @pl.when(me == 2)
            def _():
                pl.semaphore_wait(barrier, 3 + nvia)

            @pl.when(relay)
            def _():
                pl.semaphore_wait(barrier, 4)

            @pl.when((me != 2) & jnp.logical_not(relay))
            def _():
                pl.semaphore_wait(barrier, 3)
        else:
            pl.semaphore_wait(barrier, 3)

    def send_d1(r):
        if nvia:
            @pl.when((me != 2) | (r >= nvia))
            def _():
                remote(D1, r).start()
        else:
            remote(D1, r).start()

    def each(body):
        def run(r, carry):
            body(r)
            return carry
        lax.fori_loop(0, nchunks, run, 0)

    def each_tile(body):
        def run(j, carry):
            body(j)
            return carry
        lax.fori_loop(0, ntiles, run, 0)

    def gradient(step, part, source):
        two = split(source[part, :])
        uh[part, :], ul[part, :] = two
        scores = dot3(two, (ch[...], cl[...]), NT)
        ecount = e[step, part, :].astype(F32)
        resid = (ecount + w[step:step + 1, :].astype(F32)) * jax.nn.sigmoid(scores) - ecount
        two = split(resid)
        rh[part, :], rl[part, :] = two
        return dot3(two, (ch[...], cl[...]), NN)

    def contexts(step):
        def one(j):
            grad = dot3((rh[:, cols(j)], rl[:, cols(j)]), (uh[...], ul[...]), TN)
            moments = h[cols(j), :] + grad * grad
            value = c[cols(j), :] - 0.05 * grad * lax.rsqrt(moments)
            (h if step < 2 else ho)[cols(j), :] = moments
            (c if step < 2 else co)[cols(j), :] = value
            if step < 2:
                ch[cols(j), :], cl[cols(j), :] = split(value)
        each_tile(one)

    ins[0].wait()
    for r in range(1, nchunks):
        counts(0, r).start()
    ins[3].start()

    def prepare(j):
        ch[cols(j), :], cl[cols(j), :] = split(c[cols(j), :])
    each_tile(prepare)
    each(lambda r: counts(1, r).start())
    ins[1].wait()
    ins[4].wait()
    ins[2].wait()

    def first(part):
        grad = gradient(0, part, u)
        moments = g[part, :] + grad * grad
        u[part, :] = u[part, :] - 0.05 * grad * lax.rsqrt(moments)
        g[part, :] = moments

    def step0(r):
        counts(0, r).wait()
        first(rows(r))

        @pl.when(r == 0)
        def _():
            enter()
        remote(U1, r).start()

    each(step0)
    each(lambda r: counts(2, r).start())
    each(lambda r: remote(G1, r).start())
    ins[3].wait()
    contexts(0)

    def step1(r):
        remote(U1, r).wait_recv()
        counts(1, r).wait()
        out[1, rows(r), :] = gradient(1, rows(r), land.at[U1])
        if nvia:
            @pl.when((me == 2) & (r < nvia))
            def _():
                via_in(r).start()
    each(step1)

    def forward(r):
        if nvia:
            @pl.when(relay & (r == 2))
            def _():
                via_in(lax.div(me, 4) - 1).wait_recv()
                via_out(lax.div(me, 4) - 1).start()
        remote(G1, r).wait_recv()
        grad = out[1, rows(r), :]
        moments = land[G1, rows(r), :] + grad * grad
        out[0, rows(r), :] = land[U1, rows(r), :] - 0.05 * grad * lax.rsqrt(moments)
        remote(U2, r).start()
    contexts(1)
    each(forward)
    held = hold & (lax.rem(me, 4) < 2)
    free = jnp.logical_not(held)

    @pl.when(free | (lax.rem(me, 2) == 1))
    def _():
        each(send_d1)

    def step2(r):
        remote(U2, r).wait_recv()

        if hold:
            @pl.when((lax.rem(me, 4) == 2) & (r == nchunks - 4))
            def _():
                for shift in (2, 3):
                    pl.semaphore_signal(grant, inc=1, device_id=(snap, at(shift)), device_id_type=MESH)

        counts(2, r).wait()
        out[2, rows(r), :] = gradient(2, rows(r), land.at[U2])

        @pl.when(free)
        def _():
            remote(D2, r).start()
    each(step2)

    if hold:
        @pl.when(held)
        def _():
            pl.semaphore_wait(grant, 1)

            @pl.when(lax.rem(me, 2) == 0)
            def _():
                each(send_d1)
            each(lambda r: remote(D2, r).start())
    contexts(2)

    def home(r):
        remote(D1, r).wait_recv()
        grad = land[D1, rows(r), :]
        moments = g[rows(r), :] + grad * grad
        value = u[rows(r), :] - 0.05 * grad * lax.rsqrt(moments)
        remote(D2, r).wait_recv()
        grad = land[D2, rows(r), :]
        moments = moments + grad * grad
        uo[rows(r), :] = value - 0.05 * grad * lax.rsqrt(moments)
        go[rows(r), :] = moments
    each(home)

    def finish(r):
        for kind in range(5):
            remote(kind, r).wait_send()
    each(finish)
    if nvia:
        @pl.when(relay)
        def _():
            via_out(lax.div(me, 4) - 1).wait_send()


def write_out(*refs):
    copies = [pltpu.make_async_copy(refs[k], refs[4 + k], refs[8].at[k]) for k in range(4)]
    for copy in copies:
        copy.start()
    for copy in copies:
        copy.wait()


def per_device(n, vertices, vertex_moments, contexts, context_moments, edge_counts, negative_weights):
    (vb, d), cb = vertices.shape, contexts.shape[0]
    nsteps = edge_counts.shape[0]
    chunk = vb // 4 if vb % 64 == 0 else vb
    tile = cb // 2 if cb % 512 == 0 else cb
    r = vb // chunk
    hbm = pl.BlockSpec(memory_space=pltpu.HBM)
    vmem = pltpu.VMEM
    dma = pltpu.SemaphoreType.DMA
    outs = [vertices, vertex_moments, contexts, context_moments]
    limit = (64 << 20) - sum(a.size * 4 for a in outs) - (160 << 10)
    done = pl.pallas_call(
        functools.partial(kernel, n, chunk, tile),
        out_shape=[vmem(a.shape, F32) for a in outs],
        in_specs=[hbm] * 6,
        out_specs=[pl.BlockSpec(memory_space=vmem)] * 4,
        scratch_shapes=[
            vmem((vb, d), F32), vmem((vb, d), F32), vmem((cb, d), F32), vmem((cb, d), F32),
            vmem((nsteps, vb, cb), jnp.int32), vmem(negative_weights.shape, jnp.int32),
            vmem((cb, d), BF16), vmem((cb, d), BF16),
            vmem((vb, d), BF16), vmem((vb, d), BF16),
            vmem((vb, cb), BF16), vmem((vb, cb), BF16),
            vmem((5, vb, d), F32), vmem((3, vb, d), F32),
            dma((5,)), dma((nsteps, r)), dma((5, r)), dma((5, r)),
            pltpu.SemaphoreType.REGULAR, vmem((chunk, d), F32), dma((2,)),
        ],
        compiler_params=pltpu.CompilerParams(collective_id=0, has_side_effects=True, vmem_limit_bytes=limit),
    )(vertices, vertex_moments, contexts, context_moments, edge_counts, negative_weights)
    return tuple(pl.pallas_call(
        write_out,
        out_shape=[jax.ShapeDtypeStruct(a.shape, F32) for a in outs],
        in_specs=[pl.BlockSpec(memory_space=vmem)] * 4,
        out_specs=[hbm] * 4,
        scratch_shapes=[dma((4,))],
        compiler_params=pltpu.CompilerParams(vmem_limit_bytes=1 << 20),
    )(*done))


def solution(mesh):
    rows = P(("snap", "inner"), None)
    return jax.shard_map(
        functools.partial(per_device, mesh.shape["inner"]),
        mesh=mesh,
        in_specs=(rows, rows, rows, rows, P(None, None, ("snap", "inner")), P(None, ("snap", "inner"))),
        out_specs=(rows, rows, rows, rows),
        check_vma=False,
    )
```

```python
import functools

import jax
import jax.numpy as jnp
from jax import lax
from jax.experimental import pallas as pl
from jax.experimental.pallas import tpu as pltpu
from jax.sharding import PartitionSpec as P

F32 = jnp.float32
BF16 = jnp.bfloat16
MESH = pl.DeviceIdType.MESH
NN = (((1,), (0,)), ((), ()))
NT = (((1,), (1,)), ((), ()))
TN = (((0,), (0,)), ((), ()))
U1, G1, U2, D1, D2 = range(5)


def split(x):
    hi = x.astype(BF16)
    return hi, (x - hi.astype(F32)).astype(BF16)


def dot3(a, b, dims):
    dot = functools.partial(lax.dot_general, dimension_numbers=dims, preferred_element_type=F32)
    free = 1 - dims[0][0][0]
    m = a[0].shape[free]
    both = dot(jnp.concatenate(a, axis=free), b[0])
    return both[:m] + (dot(a[0], b[1]) + both[m:])


def kernel(n, chunk, tile, u_hbm, g_hbm, c_hbm, h_hbm, e_hbm, w_hbm, uo, go, co, ho,
           u, g, c, h, e, w, ch, cl, uh, ul, rh, rl, land, out,
           in_sem, e_sem, send_sem, recv_sem, grant, via, via_sem):
    me = lax.axis_index("inner")
    hold = n % 4 == 0
    nvia = max(0, min(2, u.shape[0] // chunk - 1, n // 4 - 1)) if hold else 0
    relay = (lax.rem(me, 4) == 0) & (me > 0) & (me <= 4 * nvia)
    snap = lax.axis_index("snap")
    at = lambda shift: lax.rem(me + shift + n, n)
    vb, cb = u.shape[0], c.shape[0]
    nchunks, ntiles = vb // chunk, cb // tile
    rows = lambda r: pl.ds(pl.multiple_of(r * chunk, chunk), chunk)
    cols = lambda j: pl.ds(pl.multiple_of(j * tile, tile), tile)

    ins = [pltpu.make_async_copy(src, dst, in_sem.at[k])
           for k, (src, dst) in enumerate(((c_hbm, c), (u_hbm, u), (g_hbm, g), (h_hbm, h), (w_hbm, w)))]

    def counts(step, r):
        return pltpu.make_async_copy(e_hbm.at[step, rows(r)], e.at[step, rows(r)], e_sem.at[step, r])

    ins[0].start()
    ins[1].start()
    ins[4].start()
    counts(0, 0).start()
    ins[2].start()

    barrier = pltpu.get_barrier_semaphore()
    for shift in (-1, -2, -3):
        pl.semaphore_signal(barrier, inc=1, device_id=(snap, at(shift)), device_id_type=MESH)
    if nvia:
        @pl.when(me == 1)
        def _():
            for k in range(nvia):
                pl.semaphore_signal(barrier, inc=1, device_id=(snap, 4 * (k + 1)), device_id_type=MESH)

        @pl.when(relay)
        def _():
            pl.semaphore_signal(barrier, inc=1, device_id=(snap, 2), device_id_type=MESH)

    def part_of(kind, r, part):
        src = (u, g, out.at[0], out.at[1], out.at[2])[kind]
        to = (1, 1, 1, -1, -2)[kind]
        return pltpu.make_async_remote_copy(
            src_ref=src.at[part], dst_ref=land.at[kind, part],
            send_sem=send_sem.at[kind, r], recv_sem=recv_sem.at[kind, r],
            device_id=(snap, at(to)), device_id_type=MESH)

    def remote(kind, r):
        return part_of(kind, r, rows(r))

    def via_in(r):
        return pltpu.make_async_remote_copy(
            src_ref=out.at[1, rows(r)], dst_ref=via, send_sem=send_sem.at[D1, r], recv_sem=via_sem.at[0],
            device_id=(snap, 4 * (r + 1)), device_id_type=MESH)

    def via_out(r):
        return pltpu.make_async_remote_copy(
            src_ref=via, dst_ref=land.at[D1, rows(r)], send_sem=via_sem.at[1], recv_sem=recv_sem.at[D1, r],
            device_id=(snap, 1), device_id_type=MESH)

    def enter():
        if nvia:
            @pl.when(me == 2)
            def _():
                pl.semaphore_wait(barrier, 3 + nvia)

            @pl.when(relay)
            def _():
                pl.semaphore_wait(barrier, 4)

            @pl.when((me != 2) & jnp.logical_not(relay))
            def _():
                pl.semaphore_wait(barrier, 3)
        else:
            pl.semaphore_wait(barrier, 3)

    def send_d1(r):
        if nvia:
            @pl.when((me != 2) | (r >= nvia))
            def _():
                remote(D1, r).start()
        else:
            remote(D1, r).start()

    def each(body):
        def run(r, carry):
            body(r)
            return carry
        lax.fori_loop(0, nchunks, run, 0)

    def each_tile(body):
        def run(j, carry):
            body(j)
            return carry
        lax.fori_loop(0, ntiles, run, 0)

    def gradient(step, part, source):
        two = split(source[part, :])
        uh[part, :], ul[part, :] = two
        scores = dot3(two, (ch[...], cl[...]), NT)
        ecount = e[step, part, :].astype(F32)
        resid = (ecount + w[step:step + 1, :].astype(F32)) * jax.nn.sigmoid(scores) - ecount
        two = split(resid)
        rh[part, :], rl[part, :] = two
        return dot3(two, (ch[...], cl[...]), NN)

    def contexts(step):
        def one(j):
            grad = dot3((rh[:, cols(j)], rl[:, cols(j)]), (uh[...], ul[...]), TN)
            moments = h[cols(j), :] + grad * grad
            value = c[cols(j), :] - 0.05 * grad * lax.rsqrt(moments)
            (h if step < 2 else ho)[cols(j), :] = moments
            (c if step < 2 else co)[cols(j), :] = value
            if step < 2:
                ch[cols(j), :], cl[cols(j), :] = split(value)
        each_tile(one)

    ins[0].wait()
    for r in range(1, nchunks):
        counts(0, r).start()
    ins[3].start()

    def prepare(j):
        ch[cols(j), :], cl[cols(j), :] = split(c[cols(j), :])
    each_tile(prepare)
    each(lambda r: counts(1, r).start())
    ins[1].wait()
    ins[4].wait()
    ins[2].wait()

    def first(part):
        grad = gradient(0, part, u)
        moments = g[part, :] + grad * grad
        u[part, :] = u[part, :] - 0.05 * grad * lax.rsqrt(moments)
        g[part, :] = moments

    def step0(r):
        counts(0, r).wait()
        first(rows(r))

        @pl.when(r == 0)
        def _():
            enter()
        remote(U1, r).start()

    each(step0)
    each(lambda r: counts(2, r).start())
    each(lambda r: remote(G1, r).start())
    ins[3].wait()
    contexts(0)

    early = lax.rem(me, 4) == 2

    def step1(r):
        remote(U1, r).wait_recv()
        counts(1, r).wait()
        out[1, rows(r), :] = gradient(1, rows(r), land.at[U1])
        if nvia:
            @pl.when((me == 2) & (r < nvia))
            def _():
                via_in(r).start()

        @pl.when(early)
        def _():
            send_d1(r)
    each(step1)

    def forward(r):
        if nvia:
            @pl.when(relay & (r == 2))
            def _():
                via_in(lax.div(me, 4) - 1).wait_recv()
                via_out(lax.div(me, 4) - 1).start()
        remote(G1, r).wait_recv()
        grad = out[1, rows(r), :]
        moments = land[G1, rows(r), :] + grad * grad
        out[0, rows(r), :] = land[U1, rows(r), :] - 0.05 * grad * lax.rsqrt(moments)
        remote(U2, r).start()
    contexts(1)
    each(forward)
    held = hold & (lax.rem(me, 4) < 2)
    free = jnp.logical_not(held)

    @pl.when((free | (lax.rem(me, 2) == 1)) & jnp.logical_not(early))
    def _():
        each(send_d1)

    def step2(r):
        remote(U2, r).wait_recv()

        if hold:
            @pl.when((lax.rem(me, 4) == 2) & (r == nchunks - 4))
            def _():
                for shift in (2, 3):
                    pl.semaphore_signal(grant, inc=1, device_id=(snap, at(shift)), device_id_type=MESH)

        counts(2, r).wait()
        out[2, rows(r), :] = gradient(2, rows(r), land.at[U2])

        @pl.when(free)
        def _():
            remote(D2, r).start()
    each(step2)

    if hold:
        @pl.when(held)
        def _():
            pl.semaphore_wait(grant, 1)

            @pl.when(lax.rem(me, 2) == 0)
            def _():
                each(send_d1)
            each(lambda r: remote(D2, r).start())
    contexts(2)

    def home(r):
        remote(D1, r).wait_recv()
        grad = land[D1, rows(r), :]
        moments = g[rows(r), :] + grad * grad
        value = u[rows(r), :] - 0.05 * grad * lax.rsqrt(moments)
        remote(D2, r).wait_recv()
        grad = land[D2, rows(r), :]
        moments = moments + grad * grad
        uo[rows(r), :] = value - 0.05 * grad * lax.rsqrt(moments)
        go[rows(r), :] = moments
    each(home)

    def finish(r):
        for kind in range(5):
            remote(kind, r).wait_send()
    each(finish)
    if nvia:
        @pl.when(relay)
        def _():
            via_out(lax.div(me, 4) - 1).wait_send()


def write_out(*refs):
    copies = [pltpu.make_async_copy(refs[k], refs[4 + k], refs[8].at[k]) for k in range(4)]
    for copy in copies:
        copy.start()
    for copy in copies:
        copy.wait()


def per_device(n, vertices, vertex_moments, contexts, context_moments, edge_counts, negative_weights):
    (vb, d), cb = vertices.shape, contexts.shape[0]
    nsteps = edge_counts.shape[0]
    chunk = vb // 4 if vb % 64 == 0 else vb
    tile = cb // 2 if cb % 512 == 0 else cb
    r = vb // chunk
    hbm = pl.BlockSpec(memory_space=pltpu.HBM)
    vmem = pltpu.VMEM
    dma = pltpu.SemaphoreType.DMA
    outs = [vertices, vertex_moments, contexts, context_moments]
    limit = (64 << 20) - sum(a.size * 4 for a in outs) - (160 << 10)
    done = pl.pallas_call(
        functools.partial(kernel, n, chunk, tile),
        out_shape=[vmem(a.shape, F32) for a in outs],
        in_specs=[hbm] * 6,
        out_specs=[pl.BlockSpec(memory_space=vmem)] * 4,
        scratch_shapes=[
            vmem((vb, d), F32), vmem((vb, d), F32), vmem((cb, d), F32), vmem((cb, d), F32),
            vmem((nsteps, vb, cb), jnp.int32), vmem(negative_weights.shape, jnp.int32),
            vmem((cb, d), BF16), vmem((cb, d), BF16),
            vmem((vb, d), BF16), vmem((vb, d), BF16),
            vmem((vb, cb), BF16), vmem((vb, cb), BF16),
            vmem((5, vb, d), F32), vmem((3, vb, d), F32),
            dma((5,)), dma((nsteps, r)), dma((5, r)), dma((5, r)),
            pltpu.SemaphoreType.REGULAR, vmem((chunk, d), F32), dma((2,)),
        ],
        compiler_params=pltpu.CompilerParams(collective_id=0, has_side_effects=True, vmem_limit_bytes=limit),
    )(vertices, vertex_moments, contexts, context_moments, edge_counts, negative_weights)
    return tuple(pl.pallas_call(
        write_out,
        out_shape=[jax.ShapeDtypeStruct(a.shape, F32) for a in outs],
        in_specs=[pl.BlockSpec(memory_space=vmem)] * 4,
        out_specs=[hbm] * 4,
        scratch_shapes=[dma((4,))],
        compiler_params=pltpu.CompilerParams(vmem_limit_bytes=1 << 20),
    )(*done))


def solution(mesh):
    rows = P(("snap", "inner"), None)
    return jax.shard_map(
        functools.partial(per_device, mesh.shape["inner"]),
        mesh=mesh,
        in_specs=(rows, rows, rows, rows, P(None, None, ("snap", "inner")), P(None, ("snap", "inner"))),
        out_specs=(rows, rows, rows, rows),
        check_vma=False,
    )
```

```python
import functools

import jax
import jax.numpy as jnp
from jax import lax
from jax.experimental import pallas as pl
from jax.experimental.pallas import tpu as pltpu
from jax.sharding import PartitionSpec as P

F32 = jnp.float32
BF16 = jnp.bfloat16
MESH = pl.DeviceIdType.MESH
NN = (((1,), (0,)), ((), ()))
NT = (((1,), (1,)), ((), ()))
TN = (((0,), (0,)), ((), ()))
U1, G1, U2, D1, D2 = range(5)


def split(x):
    hi = x.astype(BF16)
    return hi, (x - hi.astype(F32)).astype(BF16)


def dot3(a, b, dims):
    dot = functools.partial(lax.dot_general, dimension_numbers=dims, preferred_element_type=F32)
    free = 1 - dims[0][0][0]
    m = a[0].shape[free]
    both = dot(jnp.concatenate(a, axis=free), b[0])
    return both[:m] + (dot(a[0], b[1]) + both[m:])


def kernel(n, chunk, tile, u_hbm, g_hbm, c_hbm, h_hbm, e_hbm, w_hbm, uo, go, co, ho,
           u, g, c, h, e, w, ch, cl, uh, ul, rh, rl, land, out,
           in_sem, e_sem, send_sem, recv_sem, grant, via, via_sem):
    me = lax.axis_index("inner")
    hold = n % 4 == 0
    nvia = max(0, min(2, u.shape[0] // chunk - 1, n // 2 - 2)) if hold else 0
    nback = 2 if nvia and u.shape[0] // chunk > 2 else 0
    slot = 2 * (lax.div(me, 4) - 1) + lax.rem(me, 4)
    relay = (lax.rem(me, 4) < 2) & (me > 3) & (slot < nvia)
    snap = lax.axis_index("snap")
    at = lambda shift: lax.rem(me + shift + n, n)
    vb, cb = u.shape[0], c.shape[0]
    nchunks, ntiles = vb // chunk, cb // tile
    rows = lambda r: pl.ds(pl.multiple_of(r * chunk, chunk), chunk)
    cols = lambda j: pl.ds(pl.multiple_of(j * tile, tile), tile)

    ins = [pltpu.make_async_copy(src, dst, in_sem.at[k])
           for k, (src, dst) in enumerate(((c_hbm, c), (u_hbm, u), (g_hbm, g), (h_hbm, h), (w_hbm, w)))]

    def counts(step, r):
        return pltpu.make_async_copy(e_hbm.at[step, rows(r)], e.at[step, rows(r)], e_sem.at[step, r])

    ins[0].start()
    ins[1].start()
    ins[4].start()
    counts(0, 0).start()
    ins[2].start()

    barrier = pltpu.get_barrier_semaphore()
    for shift in (-1, -2, -3):
        pl.semaphore_signal(barrier, inc=1, device_id=(snap, at(shift)), device_id_type=MESH)
    if nvia:
        @pl.when(me == 1)
        def _():
            for k in range(nvia):
                pl.semaphore_signal(barrier, inc=1, device_id=(snap, 4 * (k // 2 + 1) + k % 2), device_id_type=MESH)

        @pl.when(relay)
        def _():
            pl.semaphore_signal(barrier, inc=1, device_id=(snap, 2), device_id_type=MESH)
    if nback:
        @pl.when(me < nback)
        def _():
            pl.semaphore_signal(barrier, inc=1, device_id=(snap, 3), device_id_type=MESH)

        @pl.when(me == 4)
        def _():
            pl.semaphore_signal(barrier, inc=1, device_id=(snap, 0), device_id_type=MESH)

    def part_of(kind, r, part):
        src = (u, g, out.at[0], out.at[1], out.at[2])[kind]
        to = (1, 1, 1, -1, -2)[kind]
        return pltpu.make_async_remote_copy(
            src_ref=src.at[part], dst_ref=land.at[kind, part],
            send_sem=send_sem.at[kind, r], recv_sem=recv_sem.at[kind, r],
            device_id=(snap, at(to)), device_id_type=MESH)

    def remote(kind, r):
        return part_of(kind, r, rows(r))

    def via_in(r):
        return pltpu.make_async_remote_copy(
            src_ref=out.at[1, rows(r)], dst_ref=via, send_sem=send_sem.at[D1, r], recv_sem=via_sem.at[0],
            device_id=(snap, 4 * (lax.div(r, 2) + 1) + lax.rem(r, 2)), device_id_type=MESH)

    def via_out(r):
        return pltpu.make_async_remote_copy(
            src_ref=via, dst_ref=land.at[D1, rows(r)], send_sem=via_sem.at[1], recv_sem=recv_sem.at[D1, r],
            device_id=(snap, 1), device_id_type=MESH)

    def back_in(r):
        return pltpu.make_async_remote_copy(
            src_ref=g.at[rows(r)], dst_ref=via, send_sem=send_sem.at[G1, r], recv_sem=via_sem.at[0],
            device_id=(snap, r), device_id_type=MESH)

    def back_out(r):
        return pltpu.make_async_remote_copy(
            src_ref=via, dst_ref=land.at[G1, rows(r)], send_sem=via_sem.at[1], recv_sem=recv_sem.at[G1, r],
            device_id=(snap, 4), device_id_type=MESH)

    def enter():
        more = ((me == 2, nvia), (relay, 1), (me == 3, nback), (me == 0, 1 if nback else 0))
        plain = jnp.logical_not(relay) & (me != 0) & (me != 2) & (me != 3)
        if nvia:
            for here, extra in more + ((plain, 0),):
                @pl.when(here)
                def _():
                    pl.semaphore_wait(barrier, 3 + extra)
        else:
            pl.semaphore_wait(barrier, 3)

    def send_g1(r):
        if nback:
            @pl.when((me != 3) | (r >= nback))
            def _():
                remote(G1, r).start()
        else:
            remote(G1, r).start()

    def send_d1(r):
        if nvia:
            @pl.when((me != 2) | (r >= nvia))
            def _():
                remote(D1, r).start()
        else:
            remote(D1, r).start()

    def each(body):
        def run(r, carry):
            body(r)
            return carry
        lax.fori_loop(0, nchunks, run, 0)

    def each_tile(body):
        def run(j, carry):
            body(j)
            return carry
        lax.fori_loop(0, ntiles, run, 0)

    def gradient(step, part, source):
        two = split(source[part, :])
        uh[part, :], ul[part, :] = two
        scores = dot3(two, (ch[...], cl[...]), NT)
        ecount = e[step, part, :].astype(F32)
        resid = (ecount + w[step:step + 1, :].astype(F32)) * jax.nn.sigmoid(scores) - ecount
        two = split(resid)
        rh[part, :], rl[part, :] = two
        return dot3(two, (ch[...], cl[...]), NN)

    def contexts(step):
        def one(j):
            grad = dot3((rh[:, cols(j)], rl[:, cols(j)]), (uh[...], ul[...]), TN)
            moments = h[cols(j), :] + grad * grad
            value = c[cols(j), :] - 0.05 * grad * lax.rsqrt(moments)
            (h if step < 2 else ho)[cols(j), :] = moments
            (c if step < 2 else co)[cols(j), :] = value
            if step < 2:
                ch[cols(j), :], cl[cols(j), :] = split(value)
        each_tile(one)

    ins[0].wait()
    for r in range(1, nchunks):
        counts(0, r).start()
    ins[3].start()

    def prepare(j):
        ch[cols(j), :], cl[cols(j), :] = split(c[cols(j), :])
    each_tile(prepare)
    each(lambda r: counts(1, r).start())
    ins[1].wait()
    ins[4].wait()
    ins[2].wait()

    def first(part):
        grad = gradient(0, part, u)
        moments = g[part, :] + grad * grad
        u[part, :] = u[part, :] - 0.05 * grad * lax.rsqrt(moments)
        g[part, :] = moments

    def step0(r):
        counts(0, r).wait()
        first(rows(r))

        @pl.when(r == 0)
        def _():
            enter()
        remote(U1, r).start()
        if nback:
            @pl.when((me == 3) & (r < nback))
            def _():
                back_in(r).start()

    each(step0)
    each(lambda r: counts(2, r).start())
    each(send_g1)
    ins[3].wait()
    contexts(0)
    if nback:
        @pl.when(me < nback)
        def _():
            back_in(me).wait_recv()
            back_out(me).start()

    early = lax.rem(me, 4) == 2

    def step1(r):
        remote(U1, r).wait_recv()
        counts(1, r).wait()
        out[1, rows(r), :] = gradient(1, rows(r), land.at[U1])
        if nvia:
            @pl.when((me == 2) & (r < nvia))
            def _():
                via_in(r).start()

        @pl.when(early)
        def _():
            send_d1(r)
    each(step1)

    def forward(r):
        if nvia:
            @pl.when(relay & (lax.rem(me, 4) == 0) & (r == 2))
            def _():
                via_in(slot).wait_recv()
                via_out(slot).start()
        remote(G1, r).wait_recv()
        grad = out[1, rows(r), :]
        moments = land[G1, rows(r), :] + grad * grad
        out[0, rows(r), :] = land[U1, rows(r), :] - 0.05 * grad * lax.rsqrt(moments)
        remote(U2, r).start()
    contexts(1)
    each(forward)
    if nvia:
        @pl.when(relay & (lax.rem(me, 4) == 1))
        def _():
            via_in(slot).wait_recv()
            via_out(slot).start()
    held = hold & (lax.rem(me, 4) < 2)
    free = jnp.logical_not(held)
    ready = max(nchunks - 2, 0)

    @pl.when((free | (lax.rem(me, 2) == 1) | (me == 0)) & jnp.logical_not(early))
    def _():
        each(send_d1)

    def step2(r):
        remote(U2, r).wait_recv()

        if hold:
            @pl.when((lax.rem(me, 4) == 2) & (r == nchunks - 4))
            def _():
                for shift in (2, 3):
                    pl.semaphore_signal(grant, inc=1, device_id=(snap, at(shift)), device_id_type=MESH)

        if hold:
            @pl.when(held & (r == ready))
            def _():
                pl.semaphore_wait(grant, 1)

                @pl.when((lax.rem(me, 2) == 0) & (me > 0))
                def _():
                    each(send_d1)

        counts(2, r).wait()
        out[2, rows(r), :] = gradient(2, rows(r), land.at[U2])

        @pl.when(free | (r > ready))
        def _():
            remote(D2, r).start()

        @pl.when(held & (r == ready))
        def _():
            for k in range(ready + 1):
                remote(D2, k).start()
    each(step2)
    contexts(2)

    def home(r):
        remote(D1, r).wait_recv()
        grad = land[D1, rows(r), :]
        moments = g[rows(r), :] + grad * grad
        value = u[rows(r), :] - 0.05 * grad * lax.rsqrt(moments)
        remote(D2, r).wait_recv()
        grad = land[D2, rows(r), :]
        moments = moments + grad * grad
        uo[rows(r), :] = value - 0.05 * grad * lax.rsqrt(moments)
        go[rows(r), :] = moments
    each(home)

    def finish(r):
        for kind in range(5):
            remote(kind, r).wait_send()
    each(finish)
    if nback:
        @pl.when(me < nback)
        def _():
            back_out(me).wait_send()
    if nvia:
        @pl.when(relay)
        def _():
            via_out(slot).wait_send()


def write_out(*refs):
    copies = [pltpu.make_async_copy(refs[k], refs[4 + k], refs[8].at[k]) for k in range(4)]
    for copy in copies:
        copy.start()
    for copy in copies:
        copy.wait()


def per_device(n, vertices, vertex_moments, contexts, context_moments, edge_counts, negative_weights):
    (vb, d), cb = vertices.shape, contexts.shape[0]
    nsteps = edge_counts.shape[0]
    chunk = vb // 4 if vb % 64 == 0 else vb
    tile = cb // 2 if cb % 512 == 0 else cb
    r = vb // chunk
    hbm = pl.BlockSpec(memory_space=pltpu.HBM)
    vmem = pltpu.VMEM
    dma = pltpu.SemaphoreType.DMA
    outs = [vertices, vertex_moments, contexts, context_moments]
    limit = (64 << 20) - sum(a.size * 4 for a in outs) - (160 << 10)
    done = pl.pallas_call(
        functools.partial(kernel, n, chunk, tile),
        out_shape=[vmem(a.shape, F32) for a in outs],
        in_specs=[hbm] * 6,
        out_specs=[pl.BlockSpec(memory_space=vmem)] * 4,
        scratch_shapes=[
            vmem((vb, d), F32), vmem((vb, d), F32), vmem((cb, d), F32), vmem((cb, d), F32),
            vmem((nsteps, vb, cb), jnp.int32), vmem(negative_weights.shape, jnp.int32),
            vmem((cb, d), BF16), vmem((cb, d), BF16),
            vmem((vb, d), BF16), vmem((vb, d), BF16),
            vmem((vb, cb), BF16), vmem((vb, cb), BF16),
            vmem((5, vb, d), F32), vmem((3, vb, d), F32),
            dma((5,)), dma((nsteps, r)), dma((5, r)), dma((5, r)),
            pltpu.SemaphoreType.REGULAR, vmem((chunk, d), F32), dma((2,)),
        ],
        compiler_params=pltpu.CompilerParams(collective_id=0, has_side_effects=True, vmem_limit_bytes=limit),
    )(vertices, vertex_moments, contexts, context_moments, edge_counts, negative_weights)
    return tuple(pl.pallas_call(
        write_out,
        out_shape=[jax.ShapeDtypeStruct(a.shape, F32) for a in outs],
        in_specs=[pl.BlockSpec(memory_space=vmem)] * 4,
        out_specs=[hbm] * 4,
        scratch_shapes=[dma((4,))],
        compiler_params=pltpu.CompilerParams(vmem_limit_bytes=1 << 20),
    )(*done))


def solution(mesh):
    rows = P(("snap", "inner"), None)
    return jax.shard_map(
        functools.partial(per_device, mesh.shape["inner"]),
        mesh=mesh,
        in_specs=(rows, rows, rows, rows, P(None, None, ("snap", "inner")), P(None, ("snap", "inner"))),
        out_specs=(rows, rows, rows, rows),
        check_vma=False,
    )
```

```python
import functools

import jax
import jax.numpy as jnp
from jax import lax
from jax.experimental import pallas as pl
from jax.experimental.pallas import tpu as pltpu
from jax.sharding import PartitionSpec as P

F32 = jnp.float32
BF16 = jnp.bfloat16
MESH = pl.DeviceIdType.MESH
NN = (((1,), (0,)), ((), ()))
NT = (((1,), (1,)), ((), ()))
TN = (((0,), (0,)), ((), ()))
U1, G1, U2, D1, D2 = range(5)


def split(x):
    hi = x.astype(BF16)
    return hi, (x - hi.astype(F32)).astype(BF16)


def dot3(a, b, dims):
    dot = functools.partial(lax.dot_general, dimension_numbers=dims, preferred_element_type=F32)
    free = 1 - dims[0][0][0]
    m = a[0].shape[free]
    both = dot(jnp.concatenate(a, axis=free), b[0])
    return both[:m] + (dot(a[0], b[1]) + both[m:])


def kernel(n, chunk, tile, u_hbm, g_hbm, c_hbm, h_hbm, e_hbm, w_hbm, uo, go, co, ho,
           u, g, c, h, e, w, ch, cl, uh, ul, rh, rl, land, out,
           in_sem, e_sem, send_sem, recv_sem, grant, via, via_sem):
    me = lax.axis_index("inner")
    hold = n % 4 == 0
    nvia = max(0, min(2, u.shape[0] // chunk - 1, n // 2 - 2)) if hold else 0
    nback = 2 if nvia and u.shape[0] // chunk > 2 else 0
    slot = 2 * (lax.div(me, 4) - 1) + lax.rem(me, 4)
    relay = (lax.rem(me, 4) < 2) & (me > 3) & (slot < nvia)
    third = nvia == 2 and n > 8 and u.shape[0] // chunk > 3 and chunk % 32 == 0
    far = (me == 8) if third else (me < 0)
    snap = lax.axis_index("snap")
    at = lambda shift: lax.rem(me + shift + n, n)
    vb, cb = u.shape[0], c.shape[0]
    nchunks, ntiles = vb // chunk, cb // tile
    rows = lambda r: pl.ds(pl.multiple_of(r * chunk, chunk), chunk)
    cols = lambda j: pl.ds(pl.multiple_of(j * tile, tile), tile)

    ins = [pltpu.make_async_copy(src, dst, in_sem.at[k])
           for k, (src, dst) in enumerate(((c_hbm, c), (u_hbm, u), (g_hbm, g), (h_hbm, h), (w_hbm, w)))]

    def counts(step, r):
        return pltpu.make_async_copy(e_hbm.at[step, rows(r)], e.at[step, rows(r)], e_sem.at[step, r])

    ins[0].start()
    ins[1].start()
    ins[4].start()
    counts(0, 0).start()
    ins[2].start()

    barrier = pltpu.get_barrier_semaphore()
    for shift in (-1, -2, -3):
        pl.semaphore_signal(barrier, inc=1, device_id=(snap, at(shift)), device_id_type=MESH)
    if nvia:
        @pl.when(me == 1)
        def _():
            for k in range(nvia + third):
                pl.semaphore_signal(barrier, inc=1, device_id=(snap, 4 * (k // 2 + 1) + k % 2), device_id_type=MESH)

        @pl.when(relay | far)
        def _():
            pl.semaphore_signal(barrier, inc=1, device_id=(snap, 2), device_id_type=MESH)
    if nback:
        @pl.when(me < nback)
        def _():
            pl.semaphore_signal(barrier, inc=1, device_id=(snap, 3), device_id_type=MESH)

        @pl.when(me == 4)
        def _():
            pl.semaphore_signal(barrier, inc=1, device_id=(snap, 0), device_id_type=MESH)

    def part_of(kind, r, part):
        src = (u, g, out.at[0], out.at[1], out.at[2])[kind]
        to = (1, 1, 1, -1, -2)[kind]
        return pltpu.make_async_remote_copy(
            src_ref=src.at[part], dst_ref=land.at[kind, part],
            send_sem=send_sem.at[kind, r], recv_sem=recv_sem.at[kind, r],
            device_id=(snap, at(to)), device_id_type=MESH)

    def remote(kind, r):
        return part_of(kind, r, rows(r))

    def via_in(r):
        return pltpu.make_async_remote_copy(
            src_ref=out.at[1, rows(r)], dst_ref=via, send_sem=send_sem.at[D1, r], recv_sem=via_sem.at[0],
            device_id=(snap, 4 * (lax.div(r, 2) + 1) + lax.rem(r, 2)), device_id_type=MESH)

    def via_out(r):
        return pltpu.make_async_remote_copy(
            src_ref=via, dst_ref=land.at[D1, rows(r)], send_sem=via_sem.at[1], recv_sem=recv_sem.at[D1, r],
            device_id=(snap, 1), device_id_type=MESH)

    upper, lower = (pl.ds(nvia * chunk + k * (chunk // 2), chunk // 2) for k in range(2))

    def far_in():
        return pltpu.make_async_remote_copy(
            src_ref=out.at[1, upper], dst_ref=via.at[pl.ds(0, chunk // 2)],
            send_sem=send_sem.at[D1, nvia], recv_sem=via_sem.at[0], device_id=(snap, 8), device_id_type=MESH)

    def far_out():
        return pltpu.make_async_remote_copy(
            src_ref=via.at[pl.ds(0, chunk // 2)], dst_ref=land.at[D1, upper],
            send_sem=via_sem.at[1], recv_sem=recv_sem.at[D1, nvia], device_id=(snap, 1), device_id_type=MESH)

    def back_in(r):
        return pltpu.make_async_remote_copy(
            src_ref=g.at[rows(r)], dst_ref=via, send_sem=send_sem.at[G1, r], recv_sem=via_sem.at[0],
            device_id=(snap, r), device_id_type=MESH)

    def back_out(r):
        return pltpu.make_async_remote_copy(
            src_ref=via, dst_ref=land.at[G1, rows(r)], send_sem=via_sem.at[1], recv_sem=recv_sem.at[G1, r],
            device_id=(snap, 4), device_id_type=MESH)

    def enter():
        more = ((me == 2, nvia + third), (relay | far, 1), (me == 3, nback), (me == 0, 1 if nback else 0))
        plain = jnp.logical_not(relay | far) & (me != 0) & (me != 2) & (me != 3)
        if nvia:
            for here, extra in more + ((plain, 0),):
                @pl.when(here)
                def _():
                    pl.semaphore_wait(barrier, 3 + extra)
        else:
            pl.semaphore_wait(barrier, 3)

    def send_g1(r):
        if nback:
            @pl.when((me != 3) | (r >= nback))
            def _():
                remote(G1, r).start()
        else:
            remote(G1, r).start()

    def send_d1(r):
        if nvia:
            @pl.when((me != 2) | (r >= nvia + third))
            def _():
                remote(D1, r).start()
        else:
            remote(D1, r).start()

    def each(body):
        def run(r, carry):
            body(r)
            return carry
        lax.fori_loop(0, nchunks, run, 0)

    def each_tile(body):
        def run(j, carry):
            body(j)
            return carry
        lax.fori_loop(0, ntiles, run, 0)

    def gradient(step, part, source):
        two = split(source[part, :])
        uh[part, :], ul[part, :] = two
        scores = dot3(two, (ch[...], cl[...]), NT)
        ecount = e[step, part, :].astype(F32)
        resid = (ecount + w[step:step + 1, :].astype(F32)) * jax.nn.sigmoid(scores) - ecount
        two = split(resid)
        rh[part, :], rl[part, :] = two
        return dot3(two, (ch[...], cl[...]), NN)

    def contexts(step):
        def one(j):
            grad = dot3((rh[:, cols(j)], rl[:, cols(j)]), (uh[...], ul[...]), TN)
            moments = h[cols(j), :] + grad * grad
            value = c[cols(j), :] - 0.05 * grad * lax.rsqrt(moments)
            (h if step < 2 else ho)[cols(j), :] = moments
            (c if step < 2 else co)[cols(j), :] = value
            if step < 2:
                ch[cols(j), :], cl[cols(j), :] = split(value)
        each_tile(one)

    ins[0].wait()
    for r in range(1, nchunks):
        counts(0, r).start()
    ins[3].start()

    def prepare(j):
        ch[cols(j), :], cl[cols(j), :] = split(c[cols(j), :])
    each_tile(prepare)
    each(lambda r: counts(1, r).start())
    ins[1].wait()
    ins[4].wait()
    ins[2].wait()

    def first(part):
        grad = gradient(0, part, u)
        moments = g[part, :] + grad * grad
        u[part, :] = u[part, :] - 0.05 * grad * lax.rsqrt(moments)
        g[part, :] = moments

    def step0(r):
        counts(0, r).wait()
        first(rows(r))

        @pl.when(r == 0)
        def _():
            enter()
        remote(U1, r).start()
        if nback:
            @pl.when((me == 3) & (r < nback))
            def _():
                back_in(r).start()

    each(step0)
    each(lambda r: counts(2, r).start())
    each(send_g1)
    ins[3].wait()
    contexts(0)
    if nback:
        @pl.when(me < nback)
        def _():
            back_in(me).wait_recv()
            back_out(me).start()

    early = lax.rem(me, 4) == 2

    def step1(r):
        remote(U1, r).wait_recv()
        counts(1, r).wait()
        out[1, rows(r), :] = gradient(1, rows(r), land.at[U1])
        if nvia:
            @pl.when((me == 2) & (r < nvia))
            def _():
                via_in(r).start()
        if third:
            @pl.when((me == 2) & (r == nvia))
            def _():
                far_in().start()
                part_of(D1, nvia, lower).start()

        @pl.when(early)
        def _():
            send_d1(r)
    each(step1)

    def forward(r):
        if nvia:
            @pl.when(relay & (lax.rem(me, 4) == 0) & (r == 2))
            def _():
                via_in(slot).wait_recv()
                via_out(slot).start()
        if third:
            @pl.when(far & (r == 3))
            def _():
                far_in().wait_recv()
                far_out().start()
        remote(G1, r).wait_recv()
        grad = out[1, rows(r), :]
        moments = land[G1, rows(r), :] + grad * grad
        out[0, rows(r), :] = land[U1, rows(r), :] - 0.05 * grad * lax.rsqrt(moments)
        remote(U2, r).start()
    contexts(1)
    each(forward)
    if nvia:
        @pl.when(relay & (lax.rem(me, 4) == 1))
        def _():
            via_in(slot).wait_recv()
            via_out(slot).start()
    held = hold & (lax.rem(me, 4) < 2)
    free = jnp.logical_not(held)
    ready = max(nchunks - 2, 0)

    @pl.when((free | (lax.rem(me, 2) == 1) | (me == 0)) & jnp.logical_not(early))
    def _():
        each(send_d1)

    def step2(r):
        remote(U2, r).wait_recv()

        if hold:
            @pl.when((lax.rem(me, 4) == 2) & (r == nchunks - 4))
            def _():
                for shift in (2, 3):
                    pl.semaphore_signal(grant, inc=1, device_id=(snap, at(shift)), device_id_type=MESH)

        if hold:
            @pl.when(held & (r == ready))
            def _():
                pl.semaphore_wait(grant, 1)

                @pl.when((lax.rem(me, 2) == 0) & (me > 0))
                def _():
                    each(send_d1)

        counts(2, r).wait()
        out[2, rows(r), :] = gradient(2, rows(r), land.at[U2])

        @pl.when(free | (r > ready))
        def _():
            remote(D2, r).start()

        @pl.when(held & (r == ready))
        def _():
            for k in range(ready + 1):
                remote(D2, k).start()
    each(step2)
    contexts(2)

    def home(r):
        remote(D1, r).wait_recv()
        grad = land[D1, rows(r), :]
        moments = g[rows(r), :] + grad * grad
        value = u[rows(r), :] - 0.05 * grad * lax.rsqrt(moments)
        remote(D2, r).wait_recv()
        grad = land[D2, rows(r), :]
        moments = moments + grad * grad
        uo[rows(r), :] = value - 0.05 * grad * lax.rsqrt(moments)
        go[rows(r), :] = moments
    each(home)

    def finish(r):
        for kind in range(5):
            remote(kind, r).wait_send()
    each(finish)
    if third:
        @pl.when(far)
        def _():
            far_out().wait_send()
    if nback:
        @pl.when(me < nback)
        def _():
            back_out(me).wait_send()
    if nvia:
        @pl.when(relay)
        def _():
            via_out(slot).wait_send()


def write_out(*refs):
    copies = [pltpu.make_async_copy(refs[k], refs[4 + k], refs[8].at[k]) for k in range(4)]
    for copy in copies:
        copy.start()
    for copy in copies:
        copy.wait()


def per_device(n, vertices, vertex_moments, contexts, context_moments, edge_counts, negative_weights):
    (vb, d), cb = vertices.shape, contexts.shape[0]
    nsteps = edge_counts.shape[0]
    chunk = vb // 4 if vb % 64 == 0 else vb
    tile = cb // 2 if cb % 512 == 0 else cb
    r = vb // chunk
    hbm = pl.BlockSpec(memory_space=pltpu.HBM)
    vmem = pltpu.VMEM
    dma = pltpu.SemaphoreType.DMA
    outs = [vertices, vertex_moments, contexts, context_moments]
    limit = (64 << 20) - sum(a.size * 4 for a in outs) - (160 << 10)
    done = pl.pallas_call(
        functools.partial(kernel, n, chunk, tile),
        out_shape=[vmem(a.shape, F32) for a in outs],
        in_specs=[hbm] * 6,
        out_specs=[pl.BlockSpec(memory_space=vmem)] * 4,
        scratch_shapes=[
            vmem((vb, d), F32), vmem((vb, d), F32), vmem((cb, d), F32), vmem((cb, d), F32),
            vmem((nsteps, vb, cb), jnp.int32), vmem(negative_weights.shape, jnp.int32),
            vmem((cb, d), BF16), vmem((cb, d), BF16),
            vmem((vb, d), BF16), vmem((vb, d), BF16),
            vmem((vb, cb), BF16), vmem((vb, cb), BF16),
            vmem((5, vb, d), F32), vmem((3, vb, d), F32),
            dma((5,)), dma((nsteps, r)), dma((5, r)), dma((5, r)),
            pltpu.SemaphoreType.REGULAR, vmem((chunk, d), F32), dma((2,)),
        ],
        compiler_params=pltpu.CompilerParams(collective_id=0, has_side_effects=True, vmem_limit_bytes=limit),
    )(vertices, vertex_moments, contexts, context_moments, edge_counts, negative_weights)
    return tuple(pl.pallas_call(
        write_out,
        out_shape=[jax.ShapeDtypeStruct(a.shape, F32) for a in outs],
        in_specs=[pl.BlockSpec(memory_space=vmem)] * 4,
        out_specs=[hbm] * 4,
        scratch_shapes=[dma((4,))],
        compiler_params=pltpu.CompilerParams(vmem_limit_bytes=1 << 20),
    )(*done))


def solution(mesh):
    rows = P(("snap", "inner"), None)
    return jax.shard_map(
        functools.partial(per_device, mesh.shape["inner"]),
        mesh=mesh,
        in_specs=(rows, rows, rows, rows, P(None, None, ("snap", "inner")), P(None, ("snap", "inner"))),
        out_specs=(rows, rows, rows, rows),
        check_vma=False,
    )
```

```python
import functools

import jax
import jax.numpy as jnp
from jax import lax
from jax.experimental import pallas as pl
from jax.experimental.pallas import tpu as pltpu
from jax.sharding import PartitionSpec as P

F32 = jnp.float32
BF16 = jnp.bfloat16
MESH = pl.DeviceIdType.MESH
NN = (((1,), (0,)), ((), ()))
NT = (((1,), (1,)), ((), ()))
TN = (((0,), (0,)), ((), ()))
U1, G1, U2, D1, D2 = range(5)


def split(x):
    hi = x.astype(BF16)
    return hi, (x - hi.astype(F32)).astype(BF16)


def dot3(a, b, dims):
    dot = functools.partial(lax.dot_general, dimension_numbers=dims, preferred_element_type=F32)
    free = 1 - dims[0][0][0]
    m = a[0].shape[free]
    both = dot(jnp.concatenate(a, axis=free), b[0])
    return both[:m] + (dot(a[0], b[1]) + both[m:])


def kernel(n, chunk, tile, u_hbm, g_hbm, c_hbm, h_hbm, e_hbm, w_hbm, uo, go, co, ho,
           u, g, c, h, e, w, ch, cl, uh, ul, rh, rl, land, out,
           in_sem, e_sem, send_sem, recv_sem, grant, via, via_sem):
    me = lax.axis_index("inner")
    hold = n % 4 == 0
    nvia = max(0, min(2, u.shape[0] // chunk - 1, n // 2 - 2)) if hold else 0
    nback = 2 if nvia and u.shape[0] // chunk > 2 else 0
    slot = 2 * (lax.div(me, 4) - 1) + lax.rem(me, 4)
    relay = (lax.rem(me, 4) < 2) & (me > 3) & (slot < nvia)
    third = nvia == 2 and n > 8 and u.shape[0] // chunk > 3 and chunk % 32 == 0
    far = (me == 8) if third else (me < 0)
    fourth = third and n > 10
    mid = (me == 10) if fourth else (me < 0)
    giver = (me == 4) if fourth else (me < 0)
    snap = lax.axis_index("snap")
    at = lambda shift: lax.rem(me + shift + n, n)
    vb, cb = u.shape[0], c.shape[0]
    nchunks, ntiles = vb // chunk, cb // tile
    rows = lambda r: pl.ds(pl.multiple_of(r * chunk, chunk), chunk)
    cols = lambda j: pl.ds(pl.multiple_of(j * tile, tile), tile)

    ins = [pltpu.make_async_copy(src, dst, in_sem.at[k])
           for k, (src, dst) in enumerate(((c_hbm, c), (u_hbm, u), (g_hbm, g), (h_hbm, h), (w_hbm, w)))]

    def counts(step, r):
        return pltpu.make_async_copy(e_hbm.at[step, rows(r)], e.at[step, rows(r)], e_sem.at[step, r])

    ins[0].start()
    ins[1].start()
    ins[4].start()
    counts(0, 0).start()
    ins[2].start()

    barrier = pltpu.get_barrier_semaphore()
    for shift in (-1, -2, -3):
        pl.semaphore_signal(barrier, inc=1, device_id=(snap, at(shift)), device_id_type=MESH)
    if nvia:
        @pl.when(me == 1)
        def _():
            for k in range(nvia + third):
                pl.semaphore_signal(barrier, inc=1, device_id=(snap, 4 * (k // 2 + 1) + k % 2), device_id_type=MESH)

        @pl.when(relay | far)
        def _():
            pl.semaphore_signal(barrier, inc=1, device_id=(snap, 2), device_id_type=MESH)
    if fourth:
        @pl.when(mid)
        def _():
            pl.semaphore_signal(barrier, inc=1, device_id=(snap, 4), device_id_type=MESH)

        @pl.when(me == 3)
        def _():
            pl.semaphore_signal(barrier, inc=1, device_id=(snap, 10), device_id_type=MESH)
    if nback:
        @pl.when(me < nback)
        def _():
            pl.semaphore_signal(barrier, inc=1, device_id=(snap, 3), device_id_type=MESH)

        @pl.when(me == 4)
        def _():
            pl.semaphore_signal(barrier, inc=1, device_id=(snap, 0), device_id_type=MESH)

    def part_of(kind, r, part):
        src = (u, g, out.at[0], out.at[1], out.at[2])[kind]
        to = (1, 1, 1, -1, -2)[kind]
        return pltpu.make_async_remote_copy(
            src_ref=src.at[part], dst_ref=land.at[kind, part],
            send_sem=send_sem.at[kind, r], recv_sem=recv_sem.at[kind, r],
            device_id=(snap, at(to)), device_id_type=MESH)

    def remote(kind, r):
        return part_of(kind, r, rows(r))

    def via_in(r):
        return pltpu.make_async_remote_copy(
            src_ref=out.at[1, rows(r)], dst_ref=via, send_sem=send_sem.at[D1, r], recv_sem=via_sem.at[0],
            device_id=(snap, 4 * (lax.div(r, 2) + 1) + lax.rem(r, 2)), device_id_type=MESH)

    def via_out(r):
        return pltpu.make_async_remote_copy(
            src_ref=via, dst_ref=land.at[D1, rows(r)], send_sem=via_sem.at[1], recv_sem=recv_sem.at[D1, r],
            device_id=(snap, 1), device_id_type=MESH)

    upper, lower = (pl.ds(nvia * chunk + k * (chunk // 2), chunk // 2) for k in range(2))

    def far_in():
        return pltpu.make_async_remote_copy(
            src_ref=out.at[1, upper], dst_ref=via.at[pl.ds(0, chunk // 2)],
            send_sem=send_sem.at[D1, nvia], recv_sem=via_sem.at[0], device_id=(snap, 8), device_id_type=MESH)

    def far_out():
        return pltpu.make_async_remote_copy(
            src_ref=via.at[pl.ds(0, chunk // 2)], dst_ref=land.at[D1, upper],
            send_sem=via_sem.at[1], recv_sem=recv_sem.at[D1, nvia], device_id=(snap, 1), device_id_type=MESH)

    def mid_in():
        return pltpu.make_async_remote_copy(
            src_ref=out.at[1, rows(0)], dst_ref=via, send_sem=send_sem.at[D1, 0], recv_sem=via_sem.at[0],
            device_id=(snap, 10), device_id_type=MESH)

    def mid_out():
        return pltpu.make_async_remote_copy(
            src_ref=via, dst_ref=land.at[D1, rows(0)], send_sem=via_sem.at[1], recv_sem=recv_sem.at[D1, 0],
            device_id=(snap, 3), device_id_type=MESH)

    def back_in(r):
        return pltpu.make_async_remote_copy(
            src_ref=g.at[rows(r)], dst_ref=via, send_sem=send_sem.at[G1, r], recv_sem=via_sem.at[0],
            device_id=(snap, r), device_id_type=MESH)

    def back_out(r):
        return pltpu.make_async_remote_copy(
            src_ref=via, dst_ref=land.at[G1, rows(r)], send_sem=via_sem.at[1], recv_sem=recv_sem.at[G1, r],
            device_id=(snap, 4), device_id_type=MESH)

    def enter():
        more = ((me == 2, nvia + third), ((relay & jnp.logical_not(giver)) | far | mid, 1), (giver, 2), (me == 3, nback), (me == 0, 1 if nback else 0))
        plain = jnp.logical_not(relay | far | mid) & (me != 0) & (me != 2) & (me != 3)
        if nvia:
            for here, extra in more + ((plain, 0),):
                @pl.when(here)
                def _():
                    pl.semaphore_wait(barrier, 3 + extra)
        else:
            pl.semaphore_wait(barrier, 3)

    def send_g1(r):
        if nback:
            @pl.when((me != 3) | (r >= nback))
            def _():
                remote(G1, r).start()
        else:
            remote(G1, r).start()

    def send_d1(r):
        if nvia:
            @pl.when(((me != 2) | (r >= nvia + third)) & (jnp.logical_not(giver) | (r > 0)))
            def _():
                remote(D1, r).start()
        else:
            remote(D1, r).start()

    def each(body):
        def run(r, carry):
            body(r)
            return carry
        lax.fori_loop(0, nchunks, run, 0)

    def each_tile(body):
        def run(j, carry):
            body(j)
            return carry
        lax.fori_loop(0, ntiles, run, 0)

    def gradient(step, part, source):
        two = split(source[part, :])
        uh[part, :], ul[part, :] = two
        scores = dot3(two, (ch[...], cl[...]), NT)
        ecount = e[step, part, :].astype(F32)
        resid = (ecount + w[step:step + 1, :].astype(F32)) * jax.nn.sigmoid(scores) - ecount
        two = split(resid)
        rh[part, :], rl[part, :] = two
        return dot3(two, (ch[...], cl[...]), NN)

    def contexts(step):
        def one(j):
            grad = dot3((rh[:, cols(j)], rl[:, cols(j)]), (uh[...], ul[...]), TN)
            moments = h[cols(j), :] + grad * grad
            value = c[cols(j), :] - 0.05 * grad * lax.rsqrt(moments)
            (h if step < 2 else ho)[cols(j), :] = moments
            (c if step < 2 else co)[cols(j), :] = value
            if step < 2:
                ch[cols(j), :], cl[cols(j), :] = split(value)
        each_tile(one)

    ins[0].wait()
    for r in range(1, nchunks):
        counts(0, r).start()
    ins[3].start()

    def prepare(j):
        ch[cols(j), :], cl[cols(j), :] = split(c[cols(j), :])
    each_tile(prepare)
    each(lambda r: counts(1, r).start())
    ins[1].wait()
    ins[4].wait()
    ins[2].wait()

    def first(part):
        grad = gradient(0, part, u)
        moments = g[part, :] + grad * grad
        u[part, :] = u[part, :] - 0.05 * grad * lax.rsqrt(moments)
        g[part, :] = moments

    def step0(r):
        counts(0, r).wait()
        first(rows(r))

        @pl.when(r == 0)
        def _():
            enter()
        remote(U1, r).start()
        if nback:
            @pl.when((me == 3) & (r < nback))
            def _():
                back_in(r).start()

    each(step0)
    each(lambda r: counts(2, r).start())
    each(send_g1)
    ins[3].wait()
    contexts(0)
    if nback:
        @pl.when(me < nback)
        def _():
            back_in(me).wait_recv()
            back_out(me).start()

    early = lax.rem(me, 4) == 2

    def step1(r):
        remote(U1, r).wait_recv()
        counts(1, r).wait()
        out[1, rows(r), :] = gradient(1, rows(r), land.at[U1])
        if nvia:
            @pl.when((me == 2) & (r < nvia))
            def _():
                via_in(r).start()
        if fourth:
            @pl.when(giver & (r == 0))
            def _():
                mid_in().start()
        if third:
            @pl.when((me == 2) & (r == nvia))
            def _():
                far_in().start()
                part_of(D1, nvia, lower).start()

        @pl.when(early)
        def _():
            send_d1(r)
    each(step1)

    def forward(r):
        if nvia:
            @pl.when(relay & (lax.rem(me, 4) == 0) & (r == 2))
            def _():
                via_in(slot).wait_recv()
                via_out(slot).start()
        if third:
            @pl.when(far & (r == 3))
            def _():
                far_in().wait_recv()
                far_out().start()
        remote(G1, r).wait_recv()
        grad = out[1, rows(r), :]
        moments = land[G1, rows(r), :] + grad * grad
        out[0, rows(r), :] = land[U1, rows(r), :] - 0.05 * grad * lax.rsqrt(moments)
        remote(U2, r).start()
    contexts(1)
    each(forward)
    if fourth:
        @pl.when(mid)
        def _():
            mid_in().wait_recv()
            mid_out().start()
    if nvia:
        @pl.when(relay & (lax.rem(me, 4) == 1))
        def _():
            via_in(slot).wait_recv()
            via_out(slot).start()
    held = hold & (lax.rem(me, 4) < 2)
    free = jnp.logical_not(held)
    ready = max(nchunks - 2, 0)

    @pl.when((free | (lax.rem(me, 2) == 1) | (me == 0)) & jnp.logical_not(early))
    def _():
        each(send_d1)

    def step2(r):
        remote(U2, r).wait_recv()

        if hold:
            @pl.when((lax.rem(me, 4) == 2) & (r == nchunks - 4))
            def _():
                for shift in (2, 3):
                    pl.semaphore_signal(grant, inc=1, device_id=(snap, at(shift)), device_id_type=MESH)

        if hold:
            @pl.when(held & (r == ready))
            def _():
                pl.semaphore_wait(grant, 1)

                @pl.when((lax.rem(me, 2) == 0) & (me > 0))
                def _():
                    each(send_d1)

        counts(2, r).wait()
        out[2, rows(r), :] = gradient(2, rows(r), land.at[U2])

        @pl.when(free | (r > ready))
        def _():
            remote(D2, r).start()

        @pl.when(held & (r == ready))
        def _():
            for k in range(ready + 1):
                remote(D2, k).start()
    each(step2)
    contexts(2)

    def home(r):
        remote(D1, r).wait_recv()
        grad = land[D1, rows(r), :]
        moments = g[rows(r), :] + grad * grad
        value = u[rows(r), :] - 0.05 * grad * lax.rsqrt(moments)
        remote(D2, r).wait_recv()
        grad = land[D2, rows(r), :]
        moments = moments + grad * grad
        uo[rows(r), :] = value - 0.05 * grad * lax.rsqrt(moments)
        go[rows(r), :] = moments
    each(home)

    def finish(r):
        for kind in range(5):
            remote(kind, r).wait_send()
    each(finish)
    if fourth:
        @pl.when(mid)
        def _():
            mid_out().wait_send()
    if third:
        @pl.when(far)
        def _():
            far_out().wait_send()
    if nback:
        @pl.when(me < nback)
        def _():
            back_out(me).wait_send()
    if nvia:
        @pl.when(relay)
        def _():
            via_out(slot).wait_send()


def write_out(*refs):
    copies = [pltpu.make_async_copy(refs[k], refs[4 + k], refs[8].at[k]) for k in range(4)]
    for copy in copies:
        copy.start()
    for copy in copies:
        copy.wait()


def per_device(n, vertices, vertex_moments, contexts, context_moments, edge_counts, negative_weights):
    (vb, d), cb = vertices.shape, contexts.shape[0]
    nsteps = edge_counts.shape[0]
    chunk = vb // 4 if vb % 64 == 0 else vb
    tile = cb // 2 if cb % 512 == 0 else cb
    r = vb // chunk
    hbm = pl.BlockSpec(memory_space=pltpu.HBM)
    vmem = pltpu.VMEM
    dma = pltpu.SemaphoreType.DMA
    outs = [vertices, vertex_moments, contexts, context_moments]
    limit = (64 << 20) - sum(a.size * 4 for a in outs) - (160 << 10)
    done = pl.pallas_call(
        functools.partial(kernel, n, chunk, tile),
        out_shape=[vmem(a.shape, F32) for a in outs],
        in_specs=[hbm] * 6,
        out_specs=[pl.BlockSpec(memory_space=vmem)] * 4,
        scratch_shapes=[
            vmem((vb, d), F32), vmem((vb, d), F32), vmem((cb, d), F32), vmem((cb, d), F32),
            vmem((nsteps, vb, cb), jnp.int32), vmem(negative_weights.shape, jnp.int32),
            vmem((cb, d), BF16), vmem((cb, d), BF16),
            vmem((vb, d), BF16), vmem((vb, d), BF16),
            vmem((vb, cb), BF16), vmem((vb, cb), BF16),
            vmem((5, vb, d), F32), vmem((3, vb, d), F32),
            dma((5,)), dma((nsteps, r)), dma((5, r)), dma((5, r)),
            pltpu.SemaphoreType.REGULAR, vmem((chunk, d), F32), dma((2,)),
        ],
        compiler_params=pltpu.CompilerParams(collective_id=0, has_side_effects=True, vmem_limit_bytes=limit),
    )(vertices, vertex_moments, contexts, context_moments, edge_counts, negative_weights)
    return tuple(pl.pallas_call(
        write_out,
        out_shape=[jax.ShapeDtypeStruct(a.shape, F32) for a in outs],
        in_specs=[pl.BlockSpec(memory_space=vmem)] * 4,
        out_specs=[hbm] * 4,
        scratch_shapes=[dma((4,))],
        compiler_params=pltpu.CompilerParams(vmem_limit_bytes=1 << 20),
    )(*done))


def solution(mesh):
    rows = P(("snap", "inner"), None)
    return jax.shard_map(
        functools.partial(per_device, mesh.shape["inner"]),
        mesh=mesh,
        in_specs=(rows, rows, rows, rows, P(None, None, ("snap", "inner")), P(None, ("snap", "inner"))),
        out_specs=(rows, rows, rows, rows),
        check_vma=False,
    )
```

```python
import functools

import jax
import jax.numpy as jnp
from jax import lax
from jax.experimental import pallas as pl
from jax.experimental.pallas import tpu as pltpu
from jax.sharding import PartitionSpec as P

F32 = jnp.float32
BF16 = jnp.bfloat16
MESH = pl.DeviceIdType.MESH
NN = (((1,), (0,)), ((), ()))
NT = (((1,), (1,)), ((), ()))
TN = (((0,), (0,)), ((), ()))
U1, G1, U2, D1, D2 = range(5)


def split(x):
    hi = x.astype(BF16)
    return hi, (x - hi.astype(F32)).astype(BF16)


def dot3(a, b, dims):
    dot = functools.partial(lax.dot_general, dimension_numbers=dims, preferred_element_type=F32)
    free = 1 - dims[0][0][0]
    m = a[0].shape[free]
    both = dot(jnp.concatenate(a, axis=free), b[0])
    return both[:m] + (dot(a[0], b[1]) + both[m:])


def kernel(n, chunk, tile, u_hbm, g_hbm, c_hbm, h_hbm, e_hbm, w_hbm, uo, go, co, ho,
           u, g, c, h, e, w, ch, cl, uh, ul, rh, rl, land, out,
           in_sem, e_sem, send_sem, recv_sem, grant, via, via_sem):
    me = lax.axis_index("inner")
    hold = n % 4 == 0
    nvia = max(0, min(2, u.shape[0] // chunk - 1, n // 2 - 2)) if hold else 0
    nback = 2 if nvia and u.shape[0] // chunk > 2 else 0
    slot = 2 * (lax.div(me, 4) - 1) + lax.rem(me, 4)
    relay = (lax.rem(me, 4) < 2) & (me > 3) & (slot < nvia)
    third = nvia == 2 and n > 8 and u.shape[0] // chunk > 3 and chunk % 32 == 0
    far = (me == 8) if third else (me < 0)
    fourth = third and n > 10
    mid = (me == 10) if fourth else (me < 0)
    giver = (me == 4) if fourth else (me < 0)
    snap = lax.axis_index("snap")
    at = lambda shift: lax.rem(me + shift + n, n)
    vb, cb = u.shape[0], c.shape[0]
    nchunks, ntiles = vb // chunk, cb // tile
    rows = lambda r: pl.ds(pl.multiple_of(r * chunk, chunk), chunk)
    cols = lambda j: pl.ds(pl.multiple_of(j * tile, tile), tile)

    ins = [pltpu.make_async_copy(src, dst, in_sem.at[k])
           for k, (src, dst) in enumerate(((c_hbm, c), (u_hbm, u), (g_hbm, g), (h_hbm, h), (w_hbm, w)))]

    def counts(step, r):
        return pltpu.make_async_copy(e_hbm.at[step, rows(r)], e.at[step, rows(r)], e_sem.at[step, r])

    ins[0].start()
    ins[1].start()
    ins[4].start()
    counts(0, 0).start()
    ins[2].start()

    barrier = pltpu.get_barrier_semaphore()
    for shift in (-1, -2, -3):
        pl.semaphore_signal(barrier, inc=1, device_id=(snap, at(shift)), device_id_type=MESH)
    if nvia:
        @pl.when(me == 1)
        def _():
            for k in range(nvia + third):
                pl.semaphore_signal(barrier, inc=1, device_id=(snap, 4 * (k // 2 + 1) + k % 2), device_id_type=MESH)

        @pl.when(relay | far)
        def _():
            pl.semaphore_signal(barrier, inc=1, device_id=(snap, 2), device_id_type=MESH)
    if fourth:
        @pl.when(mid)
        def _():
            pl.semaphore_signal(barrier, inc=1, device_id=(snap, 4), device_id_type=MESH)

        @pl.when(me == 3)
        def _():
            pl.semaphore_signal(barrier, inc=1, device_id=(snap, 10), device_id_type=MESH)
    if nback:
        @pl.when(me < nback)
        def _():
            pl.semaphore_signal(barrier, inc=1, device_id=(snap, 3), device_id_type=MESH)

        @pl.when(me == 4)
        def _():
            pl.semaphore_signal(barrier, inc=1, device_id=(snap, 0), device_id_type=MESH)

    def part_of(kind, r, part):
        src = (u, g, out.at[0], out.at[1], out.at[2])[kind]
        to = (1, 1, 1, -1, -2)[kind]
        return pltpu.make_async_remote_copy(
            src_ref=src.at[part], dst_ref=land.at[kind, part],
            send_sem=send_sem.at[kind, r], recv_sem=recv_sem.at[kind, r],
            device_id=(snap, at(to)), device_id_type=MESH)

    def remote(kind, r):
        return part_of(kind, r, rows(r))

    def via_in(r):
        return pltpu.make_async_remote_copy(
            src_ref=out.at[1, rows(r)], dst_ref=via, send_sem=send_sem.at[D1, r], recv_sem=via_sem.at[0],
            device_id=(snap, 4 * (lax.div(r, 2) + 1) + lax.rem(r, 2)), device_id_type=MESH)

    def via_out(r):
        return pltpu.make_async_remote_copy(
            src_ref=via, dst_ref=land.at[D1, rows(r)], send_sem=via_sem.at[1], recv_sem=recv_sem.at[D1, r],
            device_id=(snap, 1), device_id_type=MESH)

    most = chunk * 3 // 4
    upper, lower = pl.ds(nvia * chunk, most), pl.ds(nvia * chunk + most, chunk - most)

    def far_in():
        return pltpu.make_async_remote_copy(
            src_ref=out.at[1, upper], dst_ref=via.at[pl.ds(0, most)],
            send_sem=send_sem.at[D1, nvia], recv_sem=via_sem.at[0], device_id=(snap, 8), device_id_type=MESH)

    def far_out():
        return pltpu.make_async_remote_copy(
            src_ref=via.at[pl.ds(0, most)], dst_ref=land.at[D1, upper],
            send_sem=via_sem.at[1], recv_sem=recv_sem.at[D1, nvia], device_id=(snap, 1), device_id_type=MESH)

    def mid_in():
        return pltpu.make_async_remote_copy(
            src_ref=out.at[1, rows(0)], dst_ref=via, send_sem=send_sem.at[D1, 0], recv_sem=via_sem.at[0],
            device_id=(snap, 10), device_id_type=MESH)

    def mid_out():
        return pltpu.make_async_remote_copy(
            src_ref=via, dst_ref=land.at[D1, rows(0)], send_sem=via_sem.at[1], recv_sem=recv_sem.at[D1, 0],
            device_id=(snap, 3), device_id_type=MESH)

    def back_in(r):
        return pltpu.make_async_remote_copy(
            src_ref=g.at[rows(r)], dst_ref=via, send_sem=send_sem.at[G1, r], recv_sem=via_sem.at[0],
            device_id=(snap, r), device_id_type=MESH)

    def back_out(r):
        return pltpu.make_async_remote_copy(
            src_ref=via, dst_ref=land.at[G1, rows(r)], send_sem=via_sem.at[1], recv_sem=recv_sem.at[G1, r],
            device_id=(snap, 4), device_id_type=MESH)

    def enter():
        more = ((me == 2, nvia + third), ((relay & jnp.logical_not(giver)) | far | mid, 1), (giver, 2), (me == 3, nback), (me == 0, 1 if nback else 0))
        plain = jnp.logical_not(relay | far | mid) & (me != 0) & (me != 2) & (me != 3)
        if nvia:
            for here, extra in more + ((plain, 0),):
                @pl.when(here)
                def _():
                    pl.semaphore_wait(barrier, 3 + extra)
        else:
            pl.semaphore_wait(barrier, 3)

    def send_g1(r):
        if nback:
            @pl.when((me != 3) | (r >= nback))
            def _():
                remote(G1, r).start()
        else:
            remote(G1, r).start()

    def send_d1(r):
        if nvia:
            @pl.when(((me != 2) | (r >= nvia + third)) & (jnp.logical_not(giver) | (r > 0)))
            def _():
                remote(D1, r).start()
        else:
            remote(D1, r).start()

    def each(body):
        def run(r, carry):
            body(r)
            return carry
        lax.fori_loop(0, nchunks, run, 0)

    def each_tile(body):
        def run(j, carry):
            body(j)
            return carry
        lax.fori_loop(0, ntiles, run, 0)

    def gradient(step, part, source):
        two = split(source[part, :])
        uh[part, :], ul[part, :] = two
        scores = dot3(two, (ch[...], cl[...]), NT)
        ecount = e[step, part, :].astype(F32)
        resid = (ecount + w[step:step + 1, :].astype(F32)) * jax.nn.sigmoid(scores) - ecount
        two = split(resid)
        rh[part, :], rl[part, :] = two
        return dot3(two, (ch[...], cl[...]), NN)

    def contexts(step):
        def one(j):
            grad = dot3((rh[:, cols(j)], rl[:, cols(j)]), (uh[...], ul[...]), TN)
            moments = h[cols(j), :] + grad * grad
            value = c[cols(j), :] - 0.05 * grad * lax.rsqrt(moments)
            (h if step < 2 else ho)[cols(j), :] = moments
            (c if step < 2 else co)[cols(j), :] = value
            if step < 2:
                ch[cols(j), :], cl[cols(j), :] = split(value)
        each_tile(one)

    ins[0].wait()
    for r in range(1, nchunks):
        counts(0, r).start()
    ins[3].start()

    def prepare(j):
        ch[cols(j), :], cl[cols(j), :] = split(c[cols(j), :])
    each_tile(prepare)
    each(lambda r: counts(1, r).start())
    ins[1].wait()
    ins[4].wait()
    ins[2].wait()

    def first(part):
        grad = gradient(0, part, u)
        moments = g[part, :] + grad * grad
        u[part, :] = u[part, :] - 0.05 * grad * lax.rsqrt(moments)
        g[part, :] = moments

    def step0(r):
        counts(0, r).wait()
        first(rows(r))

        @pl.when(r == 0)
        def _():
            enter()
        remote(U1, r).start()
        if nback:
            @pl.when((me == 3) & (r < nback))
            def _():
                back_in(r).start()

    each(step0)
    each(lambda r: counts(2, r).start())
    each(send_g1)
    ins[3].wait()
    contexts(0)
    if nback:
        @pl.when(me < nback)
        def _():
            back_in(me).wait_recv()
            back_out(me).start()

    early = lax.rem(me, 4) == 2

    def step1(r):
        remote(U1, r).wait_recv()
        counts(1, r).wait()
        out[1, rows(r), :] = gradient(1, rows(r), land.at[U1])
        if nvia:
            @pl.when((me == 2) & (r < nvia))
            def _():
                via_in(r).start()
        if fourth:
            @pl.when(giver & (r == 0))
            def _():
                mid_in().start()
        if third:
            @pl.when((me == 2) & (r == nvia))
            def _():
                far_in().start()
                part_of(D1, nvia, lower).start()

        @pl.when(early)
        def _():
            send_d1(r)
    each(step1)

    def forward(r):
        if nvia:
            @pl.when(relay & (lax.rem(me, 4) == 0) & (r == 2))
            def _():
                via_in(slot).wait_recv()
                via_out(slot).start()
        if third:
            @pl.when(far & (r == 3))
            def _():
                far_in().wait_recv()
                far_out().start()
        remote(G1, r).wait_recv()
        grad = out[1, rows(r), :]
        moments = land[G1, rows(r), :] + grad * grad
        out[0, rows(r), :] = land[U1, rows(r), :] - 0.05 * grad * lax.rsqrt(moments)
        remote(U2, r).start()
    contexts(1)
    each(forward)
    if fourth:
        @pl.when(mid)
        def _():
            mid_in().wait_recv()
            mid_out().start()
    if nvia:
        @pl.when(relay & (lax.rem(me, 4) == 1))
        def _():
            via_in(slot).wait_recv()
            via_out(slot).start()
    held = hold & (lax.rem(me, 4) < 2)
    free = jnp.logical_not(held)
    ready = max(nchunks - 2, 0)

    @pl.when((free | (lax.rem(me, 2) == 1) | (me == 0)) & jnp.logical_not(early))
    def _():
        each(send_d1)

    def step2(r):
        remote(U2, r).wait_recv()

        if hold:
            @pl.when((lax.rem(me, 4) == 2) & (r == nchunks - 4))
            def _():
                for shift in (2, 3):
                    pl.semaphore_signal(grant, inc=1, device_id=(snap, at(shift)), device_id_type=MESH)

        if hold:
            @pl.when(held & (r == ready))
            def _():
                pl.semaphore_wait(grant, 1)

                @pl.when((lax.rem(me, 2) == 0) & (me > 0))
                def _():
                    each(send_d1)

        counts(2, r).wait()
        out[2, rows(r), :] = gradient(2, rows(r), land.at[U2])

        @pl.when(free | (r > ready))
        def _():
            remote(D2, r).start()

        @pl.when(held & (r == ready))
        def _():
            for k in range(ready + 1):
                remote(D2, k).start()
    each(step2)
    contexts(2)

    def home(r):
        remote(D1, r).wait_recv()
        grad = land[D1, rows(r), :]
        moments = g[rows(r), :] + grad * grad
        value = u[rows(r), :] - 0.05 * grad * lax.rsqrt(moments)
        remote(D2, r).wait_recv()
        grad = land[D2, rows(r), :]
        moments = moments + grad * grad
        uo[rows(r), :] = value - 0.05 * grad * lax.rsqrt(moments)
        go[rows(r), :] = moments
    each(home)

    def finish(r):
        for kind in range(5):
            remote(kind, r).wait_send()
    each(finish)
    if fourth:
        @pl.when(mid)
        def _():
            mid_out().wait_send()
    if third:
        @pl.when(far)
        def _():
            far_out().wait_send()
    if nback:
        @pl.when(me < nback)
        def _():
            back_out(me).wait_send()
    if nvia:
        @pl.when(relay)
        def _():
            via_out(slot).wait_send()


def write_out(*refs):
    copies = [pltpu.make_async_copy(refs[k], refs[4 + k], refs[8].at[k]) for k in range(4)]
    for copy in copies:
        copy.start()
    for copy in copies:
        copy.wait()


def per_device(n, vertices, vertex_moments, contexts, context_moments, edge_counts, negative_weights):
    (vb, d), cb = vertices.shape, contexts.shape[0]
    nsteps = edge_counts.shape[0]
    chunk = vb // 4 if vb % 64 == 0 else vb
    tile = cb // 2 if cb % 512 == 0 else cb
    r = vb // chunk
    hbm = pl.BlockSpec(memory_space=pltpu.HBM)
    vmem = pltpu.VMEM
    dma = pltpu.SemaphoreType.DMA
    outs = [vertices, vertex_moments, contexts, context_moments]
    limit = (64 << 20) - sum(a.size * 4 for a in outs) - (160 << 10)
    done = pl.pallas_call(
        functools.partial(kernel, n, chunk, tile),
        out_shape=[vmem(a.shape, F32) for a in outs],
        in_specs=[hbm] * 6,
        out_specs=[pl.BlockSpec(memory_space=vmem)] * 4,
        scratch_shapes=[
            vmem((vb, d), F32), vmem((vb, d), F32), vmem((cb, d), F32), vmem((cb, d), F32),
            vmem((nsteps, vb, cb), jnp.int32), vmem(negative_weights.shape, jnp.int32),
            vmem((cb, d), BF16), vmem((cb, d), BF16),
            vmem((vb, d), BF16), vmem((vb, d), BF16),
            vmem((vb, cb), BF16), vmem((vb, cb), BF16),
            vmem((5, vb, d), F32), vmem((3, vb, d), F32),
            dma((5,)), dma((nsteps, r)), dma((5, r)), dma((5, r)),
            pltpu.SemaphoreType.REGULAR, vmem((chunk, d), F32), dma((2,)),
        ],
        compiler_params=pltpu.CompilerParams(collective_id=0, has_side_effects=True, vmem_limit_bytes=limit),
    )(vertices, vertex_moments, contexts, context_moments, edge_counts, negative_weights)
    return tuple(pl.pallas_call(
        write_out,
        out_shape=[jax.ShapeDtypeStruct(a.shape, F32) for a in outs],
        in_specs=[pl.BlockSpec(memory_space=vmem)] * 4,
        out_specs=[hbm] * 4,
        scratch_shapes=[dma((4,))],
        compiler_params=pltpu.CompilerParams(vmem_limit_bytes=1 << 20),
    )(*done))


def solution(mesh):
    rows = P(("snap", "inner"), None)
    return jax.shard_map(
        functools.partial(per_device, mesh.shape["inner"]),
        mesh=mesh,
        in_specs=(rows, rows, rows, rows, P(None, None, ("snap", "inner")), P(None, ("snap", "inner"))),
        out_specs=(rows, rows, rows, rows),
        check_vma=False,
    )
```
